512 devices in a mesh: row: 16 (over z), col: 4 (over x_hi, core), layer: 8 (over x_lo, y).
Axes of the slice: x: 4 (x_hi: 2, x_lo: 2; x = x_hi * 2 + x_lo), y: 4, z: 16, core: 2. Of those that a mesh axis runs over, the one named last changes fastest.
Arguments:
- blocks: float32 [4096, 128, 128], P(('row', 'col', 'layer')), may hold values from -0.6 to 0.6
- block_ids: int32 [4096, 2], P(('row', 'col', 'layer')), may hold values from -1 to 1535, as said below
- out_ids: int32 [4096, 2], P(('row', 'col')), may hold values from -1 to 1535, as said below
Outputs:
- products: float32 [4096, 128, 128], P(('row', 'col', 'layer'))
The draws below stay inside these ranges and needn't reach their ends.
Inputs may be any that keep to these rules, and one draw needn't show every extreme that they name: `block_ids`: each row is the (block row, block column) of one slot, or (-1, -1) for an empty slot. The device at index (r, c, l) of (row, col, layer) holds blocks whose row is r modulo 16 and whose column is c * 8 + l modulo 4 * 8. Each row group r has between 1 and 4 block rows in use, and each column class has exactly 2 block columns in use; a device holds every block where its row group's rows in use meet its class's columns, each once, in no set order, and its other slots are empty. Some 4 + 1 row groups in a row (wrapping around) have 4 rows in use. `out_ids`: the 64 rows for the index pair (r, c) of (row, col) list, in no set order, each pair (i, j) once where i is a block row in use of row group r and j one of row group (r + 4 c + m) modulo 16 for some m < 4; the remaining rows are (-1, -1).
All inputs are finite; a program needn't handle non-finite values.
Results may differ from the reference program's by a relative error of at most 0.0003.
Values sent between devices are 32-bit elements; how exact they have to be, the bound alone decides.
No kernel may reach another device: no remote copies, remote signals or barrier semaphores. Data moves between devices by JAX's collectives and lax.ppermute only.
A program may use at most 64 MiB of HBM per device.

```python
import jax
import jax.numpy as jnp
from jax import lax

BS = 128
NB = 1536
ROWS_G = 4
COLS_DEV = 2
GRP = 4
SLOTS = 8
KALL = 64
OUT_G = 64
N_ROW = 16
N_COL = 4
N_LAYER = 8
DEVICES = 512


def pattern(key):
    base = jax.random.fold_in(key, 11)
    key_count, key_first, key_rows, key_cols = jax.random.split(base, 4)
    counts = jax.random.randint(key_count, (N_ROW,), 1, ROWS_G + 1)
    first = jax.random.randint(key_first, (), 0, N_ROW)
    offset = (jnp.arange(N_ROW) - first) % N_ROW
    counts = jnp.where(offset <= GRP, ROWS_G, counts)
    row_keys = jax.random.split(key_rows, N_ROW)
    row_span = NB // N_ROW
    picks = jax.vmap(lambda single: jax.random.permutation(single, row_span)[:ROWS_G])(row_keys)
    row_lift = jnp.where(jnp.arange(N_ROW) == N_ROW - 1, row_span - 1 - picks[:, 0], 0)
    picks = (picks + row_lift[:, None]) % row_span
    rows = picks * N_ROW + jnp.arange(N_ROW)[:, None]
    in_use = jnp.arange(ROWS_G)[None, :] < counts[:, None]
    rows = jnp.where(in_use, rows, -1)
    classes = N_COL * N_LAYER
    col_keys = jax.random.split(key_cols, classes)
    col_span = NB // classes
    col_picks = jax.vmap(lambda single: jax.random.permutation(single, col_span)[:COLS_DEV])(col_keys)
    col_lift = jnp.where(jnp.arange(classes) == classes - 1, col_span - 1 - col_picks[:, 0], 0)
    col_picks = (col_picks + col_lift[:, None]) % col_span
    cols = col_picks * classes + jnp.arange(classes)[:, None]
    return (rows, cols)


def draw_block_ids(key, part):
    rows, cols = pattern(key)
    classes = N_COL * N_LAYER
    device = jnp.arange(N_ROW * classes)
    row_group = device // classes
    col_class = device % classes
    slot = jnp.arange(SLOTS)
    row_pos = slot // COLS_DEV
    col_pos = slot % COLS_DEV
    block_row = rows[row_group][:, row_pos]
    block_col = cols[col_class][:, col_pos]
    block_col = jnp.where(block_row >= 0, block_col, -1)
    perm_keys = jax.random.split(jax.random.fold_in(key, 23), N_ROW * classes)
    orders = jax.vmap(lambda single: jax.random.permutation(single, SLOTS))(perm_keys)
    block_row = jnp.take_along_axis(block_row, orders, axis=1)
    block_col = jnp.take_along_axis(block_col, orders, axis=1)
    return jnp.stack([block_row, block_col], axis=-1).reshape(N_ROW * classes * SLOTS, 2).astype(jnp.int32)


def draw_out_ids(key, part):
    rows, cols = pattern(key)
    pair_index = jnp.arange(N_ROW * N_COL)
    row_group = pair_index // N_COL
    col_group = pair_index % N_COL
    slot = jnp.arange(OUT_G)
    left_pos = slot // (GRP * ROWS_G)
    step_pos = slot // ROWS_G % GRP
    right_pos = slot % ROWS_G
    first = rows[row_group][:, left_pos]
    other_group = (row_group[:, None] + GRP * col_group[:, None] + step_pos[None, :]) % N_ROW
    second = rows[other_group, right_pos[None, :]]
    in_use = (first >= 0) & (second >= 0)
    first = jnp.where(in_use, first, -1)
    second = jnp.where(in_use, second, -1)
    perm_keys = jax.random.split(jax.random.fold_in(key, 37), N_ROW * N_COL)
    orders = jax.vmap(lambda single: jax.random.permutation(single, OUT_G))(perm_keys)
    first = jnp.take_along_axis(first, orders, axis=1)
    second = jnp.take_along_axis(second, orders, axis=1)
    return jnp.stack([first, second], axis=-1).reshape(N_ROW * N_COL * OUT_G, 2).astype(jnp.int32)


def shard_levels(rng, extent, shards, least, top_value):
    def one(position, parts):
        heights = jax.random.uniform(jax.random.fold_in(jax.random.fold_in(rng, 6), position), (parts,), jnp.float32, least / len(shards), top_value / len(shards))
        return jnp.repeat(jnp.exp(heights), extent[position] // parts).reshape((-1,) + (1,) * (len(extent) - position - 1))

    level = one(*shards[0])
    for cut in shards[1:]:
        level = level * one(*cut)
    return level


def noise(key, shape, scale, limit, shards=(), kind=jnp.bfloat16):
    entries = scale * jax.random.normal(key, shape, jnp.float32)
    if shards:
        entries = entries * shard_levels(key, shape, shards, -0.22, 0.18)
    return jnp.clip(entries, -limit, limit).astype(kind)


def setup_inputs(seed: int = 0) -> dict:
    keys = jax.random.split(jax.random.key(seed), 4)
    blocks = noise(keys[0], (DEVICES * SLOTS, BS, BS), 0.1, 0.6, ((0, 512),), jnp.float32)
    block_ids = draw_block_ids(jax.random.fold_in(keys[3], 71), 0)
    out_ids = draw_out_ids(jax.random.fold_in(keys[3], 71), 0)
    return dict(blocks=blocks, block_ids=block_ids, out_ids=out_ids)


HIGH = lax.Precision.HIGHEST


def reference(blocks, block_ids, out_ids):
    row_ids = block_ids[:, 0]
    col_ids = block_ids[:, 1]
    held_slot = row_ids >= 0
    term_range = jnp.arange(KALL, dtype=jnp.int32)

    def single_block(out_pair):
        first = out_pair[0]
        second = out_pair[1]
        usable_pair = (first >= 0) & (second >= 0)
        left_hit = held_slot & (row_ids == first)
        left_slot = jnp.nonzero(left_hit, size=KALL, fill_value=0)[0].astype(jnp.int32)
        left_count = jnp.sum(left_hit.astype(jnp.int32))
        left_cols = jnp.take(col_ids, left_slot)
        right_hit = held_slot[None, :] & (row_ids[None, :] == second) & (col_ids[None, :] == left_cols[:, None])
        usable = jnp.any(right_hit, axis=1) & (term_range < left_count) & usable_pair
        right_slot = jnp.argmax(right_hit, axis=1).astype(jnp.int32)
        left_part = jnp.where(usable[:, None, None], jnp.take(blocks, left_slot, axis=0), jnp.float32(0.0))
        right_part = jnp.take(blocks, right_slot, axis=0)
        left_wide = jnp.transpose(left_part, (1, 0, 2)).reshape(BS, KALL * BS)
        right_wide = jnp.transpose(right_part, (1, 0, 2)).reshape(BS, KALL * BS)
        return lax.dot_general(left_wide, right_wide, (((1,), (1,)), ((), ())), precision=HIGH, preferred_element_type=jnp.float32)

    return lax.map(single_block, out_ids, batch_size=8)
```

```python
import functools

import jax
import jax.numpy as jnp
import numpy as np
from jax import lax
from jax.experimental import pallas as pl
from jax.experimental.pallas import tpu as pltpu
from jax.sharding import Mesh
from jax.sharding import PartitionSpec as P

NB = 1536
NZ = 16
AXES = ("z", "xhi", "core", "xlo", "y")
LEFT = (0, -4, 4, 1)
RIGHT = (0, 0, -4, -3)
YA, YB, XA, XB = range(4)
ORDERS = {
    (0, 0): (YA, XA, YB, XB),
    (0, 1): (XA, YB, XB, YA),
    (1, 0): (YB, XB, YA, XA),
    (1, 1): (XB, YA, XA, YB),
}


def flat(z, xhi, core, xlo, y):
    return (((z % NZ * 2 + xhi) * 2 + core) * 2 + xlo) * 4 + y


def coords():
    for z in range(NZ):
        for xhi in range(2):
            for core in range(2):
                for xlo in range(2):
                    for y in range(4):
                        yield z, xhi, core, xlo, y


def send(value, target):
    pairs = []
    for at in coords():
        to = target(*at)
        if to is not None:
            pairs.append((flat(*at), flat(*to)))
    return lax.ppermute(value, AXES, pairs)


def other_core(z, xhi, core, xlo, y):
    return z, xhi, 1 - core, xlo, y


def ring_z(z, xhi, core, xlo, y):
    return (z - 1 if core == 0 else z + 1), xhi, core, xlo, y


def across(dim, x, y):
    if dim == YA:
        return x, y ^ 1
    if dim == YB:
        return x, (3 - y)
    if dim == XA:
        return x ^ 1, y
    return 3 - x, y


def plane_step(half, step):
    def target(z, xhi, core, xlo, y):
        x, ny = across(ORDERS[core, half][step], xhi * 2 + xlo, y)
        return z, x // 2, core, x % 2, ny

    return target


def home(chunk, same):
    def target(z, xhi, core, xlo, y):
        c = ((0, 3), (1, 2))[chunk][xhi]
        if (core == c % 2) != same:
            return None
        return z + LEFT[c], xhi, c % 2, xlo, y

    return target


def dest_table():
    table = np.zeros((2, 16, 2, 16), np.int32)
    for core in range(2):
        for x in range(4):
            for y in range(4):
                for half in range(2):
                    for index in range(16):
                        nx, ny = x, y
                        for step in range(4):
                            if index >> (3 - step) & 1:
                                nx, ny = across(ORDERS[core, half][step], nx, ny)
                        table[core, x * 4 + y, half, index] = nx * 4 + ny
    return table.reshape(-1)


def sort_kernel(ids_ref, blocks_ref, out_ref, sems):
    count = blocks_ref.shape[0]
    keys = []
    for s in range(count):
        row = ids_ref[2 * s]
        keys.append(jnp.where(row >= 0, row * NB + ids_ref[2 * s + 1], 2**30 + s))
    copies = []
    for s in range(count):
        rank = jnp.int32(0)
        for o in range(count):
            if o != s:
                rank = rank + jnp.where(keys[o] < keys[s], 1, 0)
        copies.append(pltpu.make_async_copy(blocks_ref.at[s], out_ref.at[rank], sems.at[s]))
    for copy in copies:
        copy.start()
    for copy in copies:
        copy.wait()


def sort_blocks(block_ids, blocks):
    return pl.pallas_call(
        sort_kernel,
        out_shape=jax.ShapeDtypeStruct(blocks.shape, blocks.dtype),
        in_specs=[
            pl.BlockSpec(memory_space=pltpu.SMEM),
            pl.BlockSpec(memory_space=pl.ANY),
        ],
        out_specs=pl.BlockSpec(memory_space=pl.ANY),
        scratch_shapes=[pltpu.SemaphoreType.DMA((blocks.shape[0],))],
        name="sort_blocks",
    )(block_ids.reshape(-1), blocks)


def chunk_kernel(chunk, reach, where_ref, codes_ref, table_ref, *refs):
    panels = refs[: 2 + 4 * reach]
    keep0, send0, keep1, send1, hi_ref, lo_ref = refs[2 + 4 * reach :]
    core = where_ref[0]
    place = where_ref[1]

    def put(panel, row, quarter):
        for rho in range(4):
            for col in range(2):
                x = panel[2 * rho + col]
                hi = x.astype(jnp.bfloat16)
                lo = (x - hi.astype(jnp.float32)).astype(jnp.bfloat16)
                at = ((row + 4) * 4 + rho) * 2 + quarter
                hi_ref[at, :, col * 128 : (col + 1) * 128] = hi
                lo_ref[at, :, col * 128 : (col + 1) * 128] = lo

    put(panels[0], 0, core)
    put(panels[1], 0, 1 - core)
    for k in range(1, reach + 1):
        mine_a, mine_b, their_a, their_b = panels[4 * k - 2 : 4 * k + 2]
        ahead = jnp.where(core == 0, k, -k)
        put(mine_a, ahead, core)
        put(mine_b, ahead, 1 - core)
        put(their_a, -ahead, 1 - core)
        put(their_b, -ahead, core)

    lists = ((0, 3), (1, 2))[chunk]

    def product(left, right):
        total = None
        for quarter in range(2):
            lh = hi_ref[left * 2 + quarter]
            ll = lo_ref[left * 2 + quarter]
            rh = hi_ref[right * 2 + quarter]
            rl = lo_ref[right * 2 + quarter]
            for a, b in ((lh, rh), (lh, rl), (ll, rh)):
                term = lax.dot_general(
                    a, b, (((1,), (1,)), ((), ())), preferred_element_type=jnp.float32
                )
                total = term if total is None else total + term
        return total

    for half, (kept, sent) in enumerate(((keep0, send0), (keep1, send1))):
        for side, out in enumerate((kept, sent)):

            def body(index, carry, half=half, side=side, out=out):
                spot = index // 2
                dest = table_ref[(core * 16 + place) * 32 + half * 16 + side * 8 + spot]
                far = dest // 8
                layer = dest % 8
                slot = layer * 8 + core * 4 + half * 2 + index % 2
                code = codes_ref[jnp.where(far == 0, lists[0], lists[1]) * 64 + slot]
                good = code >= 0
                code = jnp.maximum(code, 0)
                left_row = jnp.where(far == 0, LEFT[lists[0]], LEFT[lists[1]])
                right_row = jnp.where(far == 0, RIGHT[lists[0]], RIGHT[lists[1]])
                left = (left_row + 4) * 4 + code // 16
                right = (right_row + 4) * 4 + code % 16
                out[index] = jnp.where(good, product(left, right), jnp.float32(0.0))
                return carry

            lax.fori_loop(0, 16, body, 0, unroll=2)


def chunk_products(chunk, reach, where, codes, table, panels):
    piece = jax.ShapeDtypeStruct((16, 128, 128), jnp.float32)
    vmem = pl.BlockSpec(memory_space=pltpu.VMEM)
    smem = pl.BlockSpec(memory_space=pltpu.SMEM)
    return pl.pallas_call(
        functools.partial(chunk_kernel, chunk, reach),
        out_shape=[piece] * 4,
        in_specs=[smem] * 3 + [vmem] * len(panels),
        out_specs=[vmem] * 4,
        scratch_shapes=[
            pltpu.VMEM((72, 128, 256), jnp.bfloat16),
            pltpu.VMEM((72, 128, 256), jnp.bfloat16),
        ],
        compiler_params=pltpu.CompilerParams(vmem_limit_bytes=40 << 20),
        name=f"products_{chunk}",
    )(where, codes, table, *panels)


def slot_codes(out_ids, row, col):
    i = out_ids[:, 0]
    j = out_ids[:, 1]
    good = (i >= 0) & (j >= 0)
    same_j = (j[None, :] == j[:, None]) & good[None, :]
    same_i = (i[None, :] == i[:, None]) & good[None, :]
    group = lax.rem(j, NZ)
    left = jnp.sum((same_j & (i[None, :] < i[:, None])).astype(jnp.int32), axis=1)
    right = jnp.sum(
        (same_i & (group[None, :] == group[:, None]) & (j[None, :] < j[:, None])).astype(jnp.int32),
        axis=1,
    )
    step = lax.rem(group - row - 4 * col + 8 * NZ, NZ)
    return jnp.where(good, left * 16 + step * 4 + right, -1)


def halve(keeps, sends):
    for step in range(4):
        received = [send(sends[h], plane_step(h, step)) for h in range(2)]
        if step == 3:
            return [keeps[h] + received[h] for h in range(2)]
        mid = keeps[0].shape[0] // 2
        sends = [keeps[h][mid:] + received[h][mid:] for h in range(2)]
        keeps = [keeps[h][:mid] + received[h][:mid] for h in range(2)]


def bring_home(chunk, halves):
    part = jnp.concatenate(halves, axis=0)
    return send(part, home(chunk, True)), send(part, home(chunk, False))


def shards(blocks, block_ids, out_ids):
    z = lax.axis_index("z")
    xhi = lax.axis_index("xhi")
    core = lax.axis_index("core")
    x = xhi * 2 + lax.axis_index("xlo")
    where = jnp.stack([core, x * 4 + lax.axis_index("y")]).astype(jnp.int32)
    table = jnp.asarray(dest_table())

    mine_a = [sort_blocks(block_ids, blocks)]
    mine_b = [send(mine_a[0], other_core)]
    their_a, their_b = [None], [None]
    for k in range(1, 5):
        mine_a.append(send(mine_a[-1], ring_z))
        mine_b.append(send(mine_b[-1], ring_z))
        their_a.append(send(mine_a[k], other_core))
        their_b.append(send(mine_b[k], other_core))

    codes = slot_codes(out_ids, z, xhi * 2 + core)

    def to_place(z, xhi, core, xlo, y):
        return z - LEFT[xhi * 2 + core], xhi, core, xlo, y

    codes = lax.all_gather(send(codes, to_place), ("xhi", "core"), axis=0, tiled=True)

    def panels(reach):
        out = [mine_a[0], mine_b[0]]
        for k in range(1, reach + 1):
            out += [mine_a[k], mine_b[k], their_a[k], their_b[k]]
        return out

    results = []
    for chunk, reach in ((0, 3), (1, 4)):
        keep0, send0, keep1, send1 = chunk_products(chunk, reach, where, codes, table, panels(reach))
        results.append(bring_home(chunk, halve([keep0, keep1], [send0, send1])))
    same = jnp.where(core == xhi, results[0][0], results[1][0])
    cross = jnp.where(core == xhi, results[0][1], results[1][1])
    first = jnp.where(core == 0, same, cross)
    second = jnp.where(core == 0, cross, same)
    layers = jnp.concatenate([first, second], axis=0)
    return layers


def solution(mesh):
    fine = Mesh(mesh.devices.reshape(16, 2, 2, 2, 4), AXES)
    return jax.shard_map(
        shards,
        mesh=fine,
        in_specs=(P(AXES, None, None), P(AXES, None), P(("z", "xhi", "core"), None)),
        out_specs=P(AXES, None, None),
        check_vma=False,
    )
```

```python
import functools

import jax
import jax.numpy as jnp
import numpy as np
from jax import lax
from jax.experimental import pallas as pl
from jax.experimental.pallas import tpu as pltpu
from jax.sharding import Mesh
from jax.sharding import PartitionSpec as P

NB = 1536
NZ = 16
AXES = ("z", "xhi", "core", "xlo", "y")
LEFT = (0, -4, 4, 1)
RIGHT = (0, 0, -4, -3)
YA, YB, XA, XB = range(4)
ORDERS = {
    (0, 0): (YA, XA, YB, XB),
    (0, 1): (XA, YB, XB, YA),
    (1, 0): (YB, XB, YA, XA),
    (1, 1): (XB, YA, XA, YB),
}


def flat(z, xhi, core, xlo, y):
    return (((z % NZ * 2 + xhi) * 2 + core) * 2 + xlo) * 4 + y


def coords():
    for z in range(NZ):
        for xhi in range(2):
            for core in range(2):
                for xlo in range(2):
                    for y in range(4):
                        yield z, xhi, core, xlo, y


def send(value, target):
    pairs = []
    for at in coords():
        to = target(*at)
        if to is not None:
            pairs.append((flat(*at), flat(*to)))
    return lax.ppermute(value, AXES, pairs)


def other_core(z, xhi, core, xlo, y):
    return z, xhi, 1 - core, xlo, y


def ring_z(z, xhi, core, xlo, y):
    return (z - 1 if core == 0 else z + 1), xhi, core, xlo, y


def across(dim, x, y):
    if dim == YA:
        return x, y ^ 1
    if dim == YB:
        return x, (3 - y)
    if dim == XA:
        return x ^ 1, y
    return 3 - x, y


def plane_step(half, step):
    def target(z, xhi, core, xlo, y):
        x, ny = across(ORDERS[core, half][step], xhi * 2 + xlo, y)
        return z, x // 2, core, x % 2, ny

    return target


def home(chunk, same):
    def target(z, xhi, core, xlo, y):
        c = ((0, 3), (1, 2))[chunk][xhi]
        if (core == c % 2) != same:
            return None
        return z + LEFT[c], xhi, c % 2, xlo, y

    return target


def dest_table():
    table = np.zeros((2, 16, 2, 16), np.int32)
    for core in range(2):
        for x in range(4):
            for y in range(4):
                for half in range(2):
                    for index in range(16):
                        nx, ny = x, y
                        for step in range(4):
                            if index >> (3 - step) & 1:
                                nx, ny = across(ORDERS[core, half][step], nx, ny)
                        table[core, x * 4 + y, half, index] = nx * 4 + ny
    return table.reshape(-1)


def sort_kernel(ids_ref, blocks_ref, out_ref):
    count = blocks_ref.shape[0]
    keys = []
    for s in range(count):
        row = ids_ref[0, s]
        keys.append(jnp.where(row >= 0, row * NB + ids_ref[1, s], 2**30 + s))
    for s in range(count):
        rank = jnp.int32(0)
        for o in range(count):
            if o != s:
                rank = rank + jnp.where(keys[o] < keys[s], 1, 0)
        out_ref[rank] = blocks_ref[s]


def sort_blocks(block_ids, blocks):
    return pl.pallas_call(
        sort_kernel,
        out_shape=jax.ShapeDtypeStruct(blocks.shape, blocks.dtype),
        in_specs=[
            pl.BlockSpec(memory_space=pltpu.SMEM),
            pl.BlockSpec(memory_space=pltpu.VMEM),
        ],
        out_specs=pl.BlockSpec(memory_space=pltpu.VMEM),
        name="sort_blocks",
    )(block_ids.T, blocks)


def chunk_kernel(chunk, reach, where_ref, codes_ref, table_ref, *refs):
    panels = refs[: 2 + 4 * reach]
    outs = refs[2 + 4 * reach : -2]
    hi_ref, lo_ref = refs[-2:]
    core = where_ref[0]
    place = where_ref[1]
    xhi = place // 8

    def put(panel, row, quarter):
        for rho in range(4):
            for col in range(2):
                x = panel[2 * rho + col]
                hi = x.astype(jnp.bfloat16)
                lo = (x - hi.astype(jnp.float32)).astype(jnp.bfloat16)
                at = ((row + 4) * 4 + rho) * 2 + quarter
                hi_ref[at, :, col * 128 : (col + 1) * 128] = hi
                lo_ref[at, :, col * 128 : (col + 1) * 128] = lo

    put(panels[0], 0, core)
    put(panels[1], 0, 1 - core)
    for k in range(1, reach + 1):
        mine_a, mine_b, their_a, their_b = panels[4 * k - 2 : 4 * k + 2]
        ahead = jnp.where(core == 0, k, -k)
        put(mine_a, ahead, core)
        put(mine_b, ahead, 1 - core)
        put(their_a, -ahead, 1 - core)
        put(their_b, -ahead, core)

    lists = ((0, 3), (1, 2))[chunk]
    held = [(c % 2 ^ core) + 2 * (c // 2 ^ xhi) for c in lists]

    def product(left, right):
        total = None
        for quarter in range(2):
            lh = hi_ref[left * 2 + quarter]
            ll = lo_ref[left * 2 + quarter]
            rh = hi_ref[right * 2 + quarter]
            rl = lo_ref[right * 2 + quarter]
            for a, b in ((lh, rh), (lh, rl), (ll, rh)):
                term = lax.dot_general(
                    a, b, (((1,), (1,)), ((), ())), preferred_element_type=jnp.float32
                )
                total = term if total is None else total + term
        return total

    def fill(out, index, dest, inner):
        far = dest // 8
        slot = dest % 8 * 8 + core * 4 + inner
        code = codes_ref[jnp.where(far == 0, held[0], held[1]), slot]
        good = code >= 0
        code = jnp.maximum(code, 0)
        left_row = jnp.where(far == 0, LEFT[lists[0]], LEFT[lists[1]])
        right_row = jnp.where(far == 0, RIGHT[lists[0]], RIGHT[lists[1]])
        left = (left_row + 4) * 4 + code // 16
        right = (right_row + 4) * 4 + code % 16
        out[index] = jnp.where(good, product(left, right), jnp.float32(0.0))

    if chunk == 0:

        def body(index, carry):
            fill(outs[0], index, index // 4, index % 4)
            return carry

        lax.fori_loop(0, 64, body, 0, unroll=2)
        return
    for half in range(2):
        for side in range(2):

            def body(index, carry, half=half, side=side):
                at = (core * 16 + place) * 32 + half * 16 + side * 8 + index // 2
                fill(outs[half * 2 + side], index, table_ref[at], half * 2 + index % 2)
                return carry

            lax.fori_loop(0, 16, body, 0, unroll=2)


def chunk_products(chunk, reach, where, codes, table, panels):
    sizes = ((64,), (16,) * 4)[chunk]
    vmem = pl.BlockSpec(memory_space=pltpu.VMEM)
    smem = pl.BlockSpec(memory_space=pltpu.SMEM)
    return pl.pallas_call(
        functools.partial(chunk_kernel, chunk, reach),
        out_shape=[jax.ShapeDtypeStruct((n, 128, 128), jnp.float32) for n in sizes],
        in_specs=[smem] * 3 + [vmem] * len(panels),
        out_specs=[vmem] * len(sizes),
        scratch_shapes=[
            pltpu.VMEM((72, 128, 256), jnp.bfloat16),
            pltpu.VMEM((72, 128, 256), jnp.bfloat16),
        ],
        compiler_params=pltpu.CompilerParams(vmem_limit_bytes=40 << 20),
        name=f"products_{chunk}",
    )(where, codes, table, *panels)


def slot_codes(out_ids, row, col):
    i = out_ids[:, 0]
    j = out_ids[:, 1]
    good = (i >= 0) & (j >= 0)
    same_j = (j[None, :] == j[:, None]) & good[None, :]
    same_i = (i[None, :] == i[:, None]) & good[None, :]
    group = lax.rem(j, NZ)
    left = jnp.sum((same_j & (i[None, :] < i[:, None])).astype(jnp.int32), axis=1)
    right = jnp.sum(
        (same_i & (group[None, :] == group[:, None]) & (j[None, :] < j[:, None])).astype(jnp.int32),
        axis=1,
    )
    step = lax.rem(group - row - 4 * col + 8 * NZ, NZ)
    return jnp.where(good, left * 16 + step * 4 + right, -1)


def halve(keeps, sends):
    for step in range(4):
        received = [send(sends[h], plane_step(h, step)) for h in range(2)]
        if step == 3:
            return [keeps[h] + received[h] for h in range(2)]
        mid = keeps[0].shape[0] // 2
        sends = [keeps[h][mid:] + received[h][mid:] for h in range(2)]
        keeps = [keeps[h][:mid] + received[h][:mid] for h in range(2)]


def bring_home(chunk, part):
    return send(part, home(chunk, True)), send(part, home(chunk, False))


def to_place(z, xhi, core, xlo, y):
    return z - LEFT[xhi * 2 + core], xhi, core, xlo, y


def other_xhi(z, xhi, core, xlo, y):
    return z, 1 - xhi, core, xlo, y


def shards(blocks, block_ids, out_ids):
    z = lax.axis_index("z")
    xhi = lax.axis_index("xhi")
    core = lax.axis_index("core")
    x = xhi * 2 + lax.axis_index("xlo")
    where = jnp.stack([core, x * 4 + lax.axis_index("y")]).astype(jnp.int32)
    table = jnp.asarray(dest_table())

    mine_a = [sort_blocks(block_ids, blocks)]
    mine_b = [send(mine_a[0], other_core)]
    their_a, their_b = [None], [None]
    for k in range(1, 5):
        mine_a.append(send(mine_a[-1], ring_z))
        mine_b.append(send(mine_b[-1], ring_z))
        their_a.append(send(mine_a[k], other_core))
        their_b.append(send(mine_b[k], other_core))

    codes = send(slot_codes(out_ids, z, xhi * 2 + core)[None], to_place)
    codes = jnp.concatenate([codes, send(codes, other_core)], axis=0)
    codes = jnp.concatenate([codes, send(codes, other_xhi)], axis=0)

    def panels(reach):
        out = [mine_a[0], mine_b[0]]
        for k in range(1, reach + 1):
            out += [mine_a[k], mine_b[k], their_a[k], their_b[k]]
        return out

    early, mine_a[4], mine_b[4] = lax.optimization_barrier((codes, mine_a[4], mine_b[4]))
    [partial] = chunk_products(0, 3, where, early, table, panels(3))
    near = lax.psum_scatter(partial, ("xhi", "xlo", "y"), scatter_dimension=0, tiled=True)
    keep0, send0, keep1, send1 = chunk_products(1, 4, where, codes, table, panels(4))
    wide = jnp.concatenate(halve([keep0, keep1], [send0, send1]), axis=0)

    same, cross = [
        jnp.where(core == xhi, a, b) for a, b in zip(bring_home(0, near), bring_home(1, wide))
    ]
    first = jnp.where(core == 0, same, cross)
    second = jnp.where(core == 0, cross, same)
    return jnp.concatenate([first, second], axis=0)


def solution(mesh):
    fine = Mesh(mesh.devices.reshape(16, 2, 2, 2, 4), AXES)
    return jax.shard_map(
        shards,
        mesh=fine,
        in_specs=(P(AXES, None, None), P(AXES, None), P(("z", "xhi", "core"), None)),
        out_specs=P(AXES, None, None),
        check_vma=False,
    )
```

```python
import functools

import jax
import jax.numpy as jnp
import numpy as np
from jax import lax
from jax.experimental import pallas as pl
from jax.experimental.pallas import tpu as pltpu
from jax.sharding import Mesh
from jax.sharding import PartitionSpec as P

NB = 1536
NZ = 16
AXES = ("z", "xhi", "core", "xlo", "y")
LEFT = (0, -4, 4, 1)
RIGHT = (0, 0, -4, -3)
YA, YB, XA, XB = range(4)
ORDERS = {
    (0, 0): (YA, XA, YB, XB),
    (0, 1): (XA, YB, XB, YA),
    (1, 0): (YB, XB, YA, XA),
    (1, 1): (XB, YA, XA, YB),
}


def flat(z, xhi, core, xlo, y):
    return (((z % NZ * 2 + xhi) * 2 + core) * 2 + xlo) * 4 + y


def coords():
    for z in range(NZ):
        for xhi in range(2):
            for core in range(2):
                for xlo in range(2):
                    for y in range(4):
                        yield z, xhi, core, xlo, y


def send(value, target):
    pairs = []
    for at in coords():
        to = target(*at)
        if to is not None:
            pairs.append((flat(*at), flat(*to)))
    return lax.ppermute(value, AXES, pairs)


def other_core(z, xhi, core, xlo, y):
    return z, xhi, 1 - core, xlo, y


def ring_z(z, xhi, core, xlo, y):
    return (z - 1 if core == 0 else z + 1), xhi, core, xlo, y


def across(dim, x, y):
    if dim == YA:
        return x, y ^ 1
    if dim == YB:
        return x, (3 - y)
    if dim == XA:
        return x ^ 1, y
    return 3 - x, y


def plane_step(half, step):
    def target(z, xhi, core, xlo, y):
        x, ny = across(ORDERS[core, half][step], xhi * 2 + xlo, y)
        return z, x // 2, core, x % 2, ny

    return target


def home(chunk, same):
    def target(z, xhi, core, xlo, y):
        c = ((0, 3), (1, 2))[chunk][xhi]
        if (core == c % 2) != same:
            return None
        return z + LEFT[c], xhi, c % 2, xlo, y

    return target


def dest_table():
    table = np.zeros((2, 16, 2, 16), np.int32)
    for core in range(2):
        for x in range(4):
            for y in range(4):
                for half in range(2):
                    for index in range(16):
                        nx, ny = x, y
                        for step in range(4):
                            if index >> (3 - step) & 1:
                                nx, ny = across(ORDERS[core, half][step], nx, ny)
                        table[core, x * 4 + y, half, index] = nx * 4 + ny
    return table.reshape(-1)


def sort_kernel(ids_ref, blocks_ref, out_ref):
    count = blocks_ref.shape[0]
    keys = []
    for s in range(count):
        row = ids_ref[0, s]
        keys.append(jnp.where(row >= 0, row * NB + ids_ref[1, s], 2**30 + s))
    for s in range(count):
        rank = jnp.int32(0)
        for o in range(count):
            if o != s:
                rank = rank + jnp.where(keys[o] < keys[s], 1, 0)
        out_ref[rank] = blocks_ref[s]


def sort_blocks(block_ids, blocks):
    return pl.pallas_call(
        sort_kernel,
        out_shape=jax.ShapeDtypeStruct(blocks.shape, blocks.dtype),
        in_specs=[
            pl.BlockSpec(memory_space=pltpu.SMEM),
            pl.BlockSpec(memory_space=pltpu.VMEM),
        ],
        out_specs=pl.BlockSpec(memory_space=pltpu.VMEM),
        name="sort_blocks",
    )(block_ids.T, blocks)


NEAR = 3


def split_into(panel, at, quarter, hi_ref, lo_ref):
    for rho in range(4):
        for col in range(2):
            x = panel[2 * rho + col]
            hi = x.astype(jnp.bfloat16)
            lo = (x - hi.astype(jnp.float32)).astype(jnp.bfloat16)
            lanes = pl.ds(pl.multiple_of(quarter * 256 + col * 128, 128), 128)
            hi_ref[at, rho * 128 : (rho + 1) * 128, lanes] = hi
            lo_ref[at, rho * 128 : (rho + 1) * 128, lanes] = lo


def split_pair(core, panels, hi_ref, lo_ref):
    ahead = 1 - core
    places = ((ahead, core), (ahead, 1 - core), (1 - ahead, 1 - core), (1 - ahead, core))
    for panel, (at, quarter) in zip(panels, places):
        split_into(panel, at, quarter, hi_ref, lo_ref)


def split_kernel(where_ref, *refs):
    core = where_ref[0]
    *panels, hi_ref, lo_ref = refs
    if len(panels) == 2:
        split_into(panels[0], 0, core, hi_ref, lo_ref)
        split_into(panels[1], 0, 1 - core, hi_ref, lo_ref)
    else:
        split_pair(core, panels, hi_ref, lo_ref)


def split_rows(where, *panels):
    vmem = pl.BlockSpec(memory_space=pltpu.VMEM)
    smem = pl.BlockSpec(memory_space=pltpu.SMEM)
    return pl.pallas_call(
        split_kernel,
        out_shape=[jax.ShapeDtypeStruct((len(panels) // 2, 512, 512), jnp.bfloat16)] * 2,
        in_specs=[smem] + [vmem] * len(panels),
        out_specs=[vmem] * 2,
        compiler_params=pltpu.CompilerParams(vmem_limit_bytes=8 << 20),
        name=f"split_{len(panels)}",
    )(where, *panels)


def chunk_kernel(chunk, where_ref, codes_ref, table_ref, *refs):
    core = where_ref[0]
    place = where_ref[1]
    xhi = place // 8
    rows_hi, rows_lo = list(refs[: 2 * NEAR + 2 : 2]), list(refs[1 : 2 * NEAR + 2 : 2])
    refs = refs[2 * NEAR + 2 :]
    if chunk == 1:
        panels, outs = refs[:4], refs[4:8]
        res_ref, far_hi, far_lo = refs[8:]
        split_pair(core, panels, far_hi, far_lo)
        rows_hi.append(far_hi)
        rows_lo.append(far_lo)
    else:
        outs = refs[:4]
        [res_ref] = refs[4:]

    def row(offset):
        at = int(offset > 0)
        return rows_hi[abs(offset)].at[at], rows_lo[abs(offset)].at[at]

    def times(a, b):
        return lax.dot_general(
            a[...], b[...], (((1,), (1,)), ((), ())), preferred_element_type=jnp.float32
        )

    lists = ((0, 3), (1, 2))[chunk]
    held = [(c % 2 ^ core) + 2 * (c // 2 ^ xhi) for c in lists]
    for far, c in enumerate(lists):
        left_hi, left_lo = row(LEFT[c])
        for step in range(4):
            right_hi, right_lo = row(RIGHT[c] + step)
            res_ref[far * 4 + step] = (
                times(left_hi, right_hi) + times(left_hi, right_lo) + times(left_lo, right_hi)
            )
    for half in range(2):
        for side in range(2):

            def pick(index, carry, half=half, side=side):
                at = (core * 16 + place) * 32 + half * 16 + side * 8 + index // 2
                dest = table_ref[at]
                far = dest // 8
                slot = dest % 8 * 8 + core * 4 + half * 2 + index % 2
                code = codes_ref[jnp.where(far == 0, held[0], held[1]), slot]
                good = code >= 0
                code = jnp.maximum(code, 0)
                rows = pl.ds(pl.multiple_of(code // 16 * 128, 128), 128)
                cols = pl.ds(pl.multiple_of(code % 4 * 128, 128), 128)
                block = res_ref[far * 4 + code // 4 % 4, rows, cols]
                outs[half * 2 + side][index] = jnp.where(good, block, jnp.float32(0.0))
                return carry

            lax.fori_loop(0, 16, pick, 0, unroll=4)


def chunk_products(chunk, where, codes, table, split, panels):
    vmem = pl.BlockSpec(memory_space=pltpu.VMEM)
    smem = pl.BlockSpec(memory_space=pltpu.SMEM)
    scratch = [pltpu.VMEM((8, 512, 512), jnp.float32)]
    if chunk == 1:
        scratch += [pltpu.VMEM((2, 512, 512), jnp.bfloat16)] * 2
    return pl.pallas_call(
        functools.partial(chunk_kernel, chunk),
        out_shape=[jax.ShapeDtypeStruct((16, 128, 128), jnp.float32)] * 4,
        in_specs=[smem] * 3 + [vmem] * (len(split) + len(panels)),
        out_specs=[vmem] * 4,
        scratch_shapes=scratch,
        compiler_params=pltpu.CompilerParams(vmem_limit_bytes=20 << 20),
        name=f"products_{chunk}",
    )(where, codes, table, *split, *panels)


def slot_codes(out_ids, row, col):
    i = out_ids[:, 0]
    j = out_ids[:, 1]
    good = (i >= 0) & (j >= 0)
    same_j = (j[None, :] == j[:, None]) & good[None, :]
    same_i = (i[None, :] == i[:, None]) & good[None, :]
    group = lax.rem(j, NZ)
    left = jnp.sum((same_j & (i[None, :] < i[:, None])).astype(jnp.int32), axis=1)
    right = jnp.sum(
        (same_i & (group[None, :] == group[:, None]) & (j[None, :] < j[:, None])).astype(jnp.int32),
        axis=1,
    )
    step = lax.rem(group - row - 4 * col + 8 * NZ, NZ)
    return jnp.where(good, left * 16 + step * 4 + right, -1)


def after(value, *others):
    return lax.optimization_barrier((value, *others))[0]


def halve(keeps, sends, others=((), (), (), ())):
    arrived = []
    for step in range(4):
        received = [
            send(after(sends[h], *others[step]) if others[step] else sends[h], plane_step(h, step))
            for h in range(2)
        ]
        arrived.append(received)
        if step == 3:
            return [keeps[h] + received[h] for h in range(2)], arrived
        mid = keeps[0].shape[0] // 2
        sends = [keeps[h][mid:] + received[h][mid:] for h in range(2)]
        keeps = [keeps[h][:mid] + received[h][:mid] for h in range(2)]


def bring_home(chunk, part):
    return send(part, home(chunk, True)), send(part, home(chunk, False))


def to_place(z, xhi, core, xlo, y):
    return z - LEFT[xhi * 2 + core], xhi, core, xlo, y


def other_xhi(z, xhi, core, xlo, y):
    return z, 1 - xhi, core, xlo, y


def shards(blocks, block_ids, out_ids):
    z = lax.axis_index("z")
    xhi = lax.axis_index("xhi")
    core = lax.axis_index("core")
    x = xhi * 2 + lax.axis_index("xlo")
    where = jnp.stack([core, x * 4 + lax.axis_index("y")]).astype(jnp.int32)
    table = jnp.asarray(dest_table())

    codes = send(slot_codes(out_ids, z, xhi * 2 + core)[None], to_place)
    codes = jnp.concatenate([codes, send(codes, other_core)], axis=0)
    codes = jnp.concatenate([codes, send(codes, other_xhi)], axis=0)

    mine_a = [sort_blocks(block_ids, blocks)]
    mine_b = [send(mine_a[0], other_core)]
    split = [split_rows(where, mine_a[0], mine_b[0])]
    their_a, their_b = [None], [None]
    for k in range(1, 5):
        next_a, next_b = mine_a[-1], mine_b[-1]
        if k == 2:
            next_a = after(next_a, codes)
        if k > 2:
            next_a = after(next_a, their_a[k - 2])
            next_b = after(next_b, split[k - 2][0])
        mine_a.append(send(next_a, ring_z))
        mine_b.append(send(next_b, ring_z))
        swap_a = mine_a[k] if k <= NEAR else after(mine_a[k], split[k - 1][0])
        their_a.append(send(swap_a, other_core))
        their_b.append(send(mine_b[k], other_core))
        if k <= NEAR:
            split.append(split_rows(where, mine_a[k], mine_b[k], their_a[k], their_b[k]))
    split = [part for pair in split for part in pair]

    keep0, send0, keep1, send1 = chunk_products(
        1, where, codes, table, split, [mine_a[4], mine_b[4], their_a[4], their_b[4]]
    )
    parts, arrived = halve([keep0, keep1], [send0, send1])
    far_home = bring_home(1, jnp.concatenate(parts, axis=0))
    first_codes = after(codes, keep0)
    keep0, send0, keep1, send1 = chunk_products(0, where, first_codes, table, split, [])
    parts, _ = halve([keep0, keep1], [send0, send1], ((), arrived[2], arrived[3], ()))
    near_home = bring_home(0, jnp.concatenate(parts, axis=0))

    same, cross = [jnp.where(core == xhi, a, b) for a, b in zip(near_home, far_home)]
    first = jnp.where(core == 0, same, cross)
    second = jnp.where(core == 0, cross, same)
    return jnp.concatenate([first, second], axis=0)


def solution(mesh):
    fine = Mesh(mesh.devices.reshape(16, 2, 2, 2, 4), AXES)
    return jax.shard_map(
        shards,
        mesh=fine,
        in_specs=(P(AXES, None, None), P(AXES, None), P(("z", "xhi", "core"), None)),
        out_specs=P(AXES, None, None),
        check_vma=False,
    )
```

```python
import functools

import jax
import jax.numpy as jnp
from jax import lax
from jax.experimental import pallas as pl
from jax.experimental.pallas import tpu as pltpu
from jax.sharding import Mesh
from jax.sharding import PartitionSpec as P

NB = 1536
NZ = 16
AXES = ("z", "xhi", "core", "xlo", "y")
LEFT = (0, -4, 4, 1)
RIGHT = (0, 0, -4, -3)


def flat(z, xhi, core, xlo, y):
    return (((z % NZ * 2 + xhi) * 2 + core) * 2 + xlo) * 4 + y


def coords():
    for z in range(NZ):
        for xhi in range(2):
            for core in range(2):
                for xlo in range(2):
                    for y in range(4):
                        yield z, xhi, core, xlo, y


def send(value, target):
    pairs = []
    for at in coords():
        to = target(*at)
        if to is not None:
            pairs.append((flat(*at), flat(*to)))
    return lax.ppermute(value, AXES, pairs)


def other_core(z, xhi, core, xlo, y):
    return z, xhi, 1 - core, xlo, y


def ring_z(z, xhi, core, xlo, y):
    return (z - 1 if core == 0 else z + 1), xhi, core, xlo, y


def plane_step(phase, offset):
    def target(z, xhi, core, xlo, y):
        if phase == core:
            return z, xhi, core, xlo, (y + offset) % 4
        x = (xhi * 2 + xlo + offset) % 4
        return z, x // 2, core, x % 2, y

    return target


def home(chunk, same):
    def target(z, xhi, core, xlo, y):
        c = ((0, 3), (1, 2))[chunk][xhi]
        if (core == c % 2) != same:
            return None
        return z + LEFT[c], xhi, c % 2, xlo, y

    return target


def sort_kernel(ids_ref, blocks_ref, out_ref):
    count = blocks_ref.shape[0]
    keys = []
    for s in range(count):
        row = ids_ref[0, s]
        keys.append(jnp.where(row >= 0, row * NB + ids_ref[1, s], 2**30 + s))
    for s in range(count):
        rank = jnp.int32(0)
        for o in range(count):
            if o != s:
                rank = rank + jnp.where(keys[o] < keys[s], 1, 0)
        out_ref[rank] = blocks_ref[s]


def sort_blocks(block_ids, blocks):
    return pl.pallas_call(
        sort_kernel,
        out_shape=jax.ShapeDtypeStruct(blocks.shape, blocks.dtype),
        in_specs=[
            pl.BlockSpec(memory_space=pltpu.SMEM),
            pl.BlockSpec(memory_space=pltpu.VMEM),
        ],
        out_specs=pl.BlockSpec(memory_space=pltpu.VMEM),
        name="sort_blocks",
    )(block_ids.T, blocks)


NEAR = 3


def split_into(panel, at, quarter, hi_ref, lo_ref):
    for rho in range(4):
        for col in range(2):
            x = panel[2 * rho + col]
            hi = x.astype(jnp.bfloat16)
            lo = (x - hi.astype(jnp.float32)).astype(jnp.bfloat16)
            lanes = pl.ds(pl.multiple_of(quarter * 256 + col * 128, 128), 128)
            hi_ref[at, rho * 128 : (rho + 1) * 128, lanes] = hi
            lo_ref[at, rho * 128 : (rho + 1) * 128, lanes] = lo


def split_pair(core, panels, hi_ref, lo_ref):
    ahead = 1 - core
    places = ((ahead, core), (ahead, 1 - core), (1 - ahead, 1 - core), (1 - ahead, core))
    for panel, (at, quarter) in zip(panels, places):
        split_into(panel, at, quarter, hi_ref, lo_ref)


def split_kernel(where_ref, *refs):
    core = where_ref[0]
    *panels, hi_ref, lo_ref = refs
    if len(panels) == 2:
        split_into(panels[0], 0, core, hi_ref, lo_ref)
        split_into(panels[1], 0, 1 - core, hi_ref, lo_ref)
    else:
        split_pair(core, panels, hi_ref, lo_ref)


def split_rows(where, *panels):
    vmem = pl.BlockSpec(memory_space=pltpu.VMEM)
    smem = pl.BlockSpec(memory_space=pltpu.SMEM)
    return pl.pallas_call(
        split_kernel,
        out_shape=[jax.ShapeDtypeStruct((len(panels) // 2, 512, 512), jnp.bfloat16)] * 2,
        in_specs=[smem] + [vmem] * len(panels),
        out_specs=[vmem] * 2,
        compiler_params=pltpu.CompilerParams(vmem_limit_bytes=8 << 20),
        name=f"split_{len(panels)}",
    )(where, *panels)


def chunk_kernel(chunk, where_ref, codes_ref, *refs):
    core = where_ref[0]
    place = where_ref[1]
    xhi = place // 8
    rows_hi, rows_lo = list(refs[: 2 * NEAR + 2 : 2]), list(refs[1 : 2 * NEAR + 2 : 2])
    refs = refs[2 * NEAR + 2 :]
    if chunk == 1:
        panels, outs = refs[:4], refs[4:8]
        res_ref, far_hi, far_lo = refs[8:]
        split_pair(core, panels, far_hi, far_lo)
        rows_hi.append(far_hi)
        rows_lo.append(far_lo)
    else:
        outs = refs[:4]
        [res_ref] = refs[4:]

    def row(offset):
        at = int(offset > 0)
        return rows_hi[abs(offset)].at[at], rows_lo[abs(offset)].at[at]

    def times(a, b):
        return lax.dot_general(
            a[...], b[...], (((1,), (1,)), ((), ())), preferred_element_type=jnp.float32
        )

    lists = ((0, 3), (1, 2))[chunk]
    held = [(c % 2 ^ core) + 2 * (c // 2 ^ xhi) for c in lists]
    for far, c in enumerate(lists):
        left_hi, left_lo = row(LEFT[c])
        for step in range(4):
            right_hi, right_lo = row(RIGHT[c] + step)
            res_ref[far * 4 + step] = (
                times(left_hi, right_hi) + times(left_hi, right_lo) + times(left_lo, right_hi)
            )
    x, y = place // 4, place % 4
    for offset in range(4):

        def pick(index, carry, offset=offset):
            after_that = index // 4
            to_x = (x + jnp.where(core == 0, after_that, offset)) % 4
            to_y = (y + jnp.where(core == 0, offset, after_that)) % 4
            far = to_x // 2
            slot = (to_x % 2 * 4 + to_y) * 8 + core * 4 + index % 4
            code = codes_ref[jnp.where(far == 0, held[0], held[1]), slot]
            good = code >= 0
            code = jnp.maximum(code, 0)
            rows = pl.ds(pl.multiple_of(code // 16 * 128, 128), 128)
            cols = pl.ds(pl.multiple_of(code % 4 * 128, 128), 128)
            block = res_ref[far * 4 + code // 4 % 4, rows, cols]
            outs[offset][index] = jnp.where(good, block, jnp.float32(0.0))
            return carry

        lax.fori_loop(0, 16, pick, 0, unroll=4)


def chunk_products(chunk, where, codes, split, panels):
    vmem = pl.BlockSpec(memory_space=pltpu.VMEM)
    smem = pl.BlockSpec(memory_space=pltpu.SMEM)
    scratch = [pltpu.VMEM((8, 512, 512), jnp.float32)]
    if chunk == 1:
        scratch += [pltpu.VMEM((2, 512, 512), jnp.bfloat16)] * 2
    return pl.pallas_call(
        functools.partial(chunk_kernel, chunk),
        out_shape=[jax.ShapeDtypeStruct((16, 128, 128), jnp.float32)] * 4,
        in_specs=[smem] * 2 + [vmem] * (len(split) + len(panels)),
        out_specs=[vmem] * 4,
        scratch_shapes=scratch,
        compiler_params=pltpu.CompilerParams(vmem_limit_bytes=20 << 20),
        name=f"products_{chunk}",
    )(where, codes, *split, *panels)


def slot_codes(out_ids, row, col):
    i = out_ids[:, 0]
    j = out_ids[:, 1]
    good = (i >= 0) & (j >= 0)
    same_j = (j[None, :] == j[:, None]) & good[None, :]
    same_i = (i[None, :] == i[:, None]) & good[None, :]
    group = lax.rem(j, NZ)
    left = jnp.sum((same_j & (i[None, :] < i[:, None])).astype(jnp.int32), axis=1)
    right = jnp.sum(
        (same_i & (group[None, :] == group[:, None]) & (j[None, :] < j[:, None])).astype(jnp.int32),
        axis=1,
    )
    step = lax.rem(group - row - 4 * col + 8 * NZ, NZ)
    return jnp.where(good, left * 16 + step * 4 + right, -1)


def after(value, *others):
    return lax.optimization_barrier((value, *others))[0]


def reduce_plane(pieces, others=()):
    received = [None] * 4
    for offset in (2, 1, 3):
        received[offset] = send(pieces[offset], plane_step(0, offset))
    if others:
        received[1:] = lax.optimization_barrier((*received[1:], *others))[:3]
    count = pieces[0].shape[0] // 4
    total = [
        sum((received[o][n * count : (n + 1) * count] for o in (1, 2, 3)), pieces[0][n * count : (n + 1) * count])
        for n in range(4)
    ]
    arrived = [send(total[offset], plane_step(1, offset)) for offset in (2, 1, 3)]
    return total[0] + arrived[0] + arrived[1] + arrived[2], arrived


def bring_home(chunk, part):
    return send(part, home(chunk, True)), send(part, home(chunk, False))


def to_place(z, xhi, core, xlo, y):
    return z - LEFT[xhi * 2 + core], xhi, core, xlo, y


def other_xhi(z, xhi, core, xlo, y):
    return z, 1 - xhi, core, xlo, y


def shards(blocks, block_ids, out_ids):
    z = lax.axis_index("z")
    xhi = lax.axis_index("xhi")
    core = lax.axis_index("core")
    x = xhi * 2 + lax.axis_index("xlo")
    where = jnp.stack([core, x * 4 + lax.axis_index("y")]).astype(jnp.int32)

    codes = send(slot_codes(out_ids, z, xhi * 2 + core)[None], to_place)
    codes = jnp.concatenate([codes, send(codes, other_core)], axis=0)
    codes = jnp.concatenate([codes, send(codes, other_xhi)], axis=0)

    mine_a = [sort_blocks(block_ids, blocks)]
    mine_b = [send(mine_a[0], other_core)]
    split = [split_rows(where, mine_a[0], mine_b[0])]
    their_a, their_b = [None], [None]
    for k in range(1, 5):
        next_a, next_b = mine_a[-1], mine_b[-1]
        if k > 2:
            next_a = after(next_a, their_a[k - 2])
            next_b = after(next_b, split[k - 2][0])
        if k == 4:
            next_a = after(next_a, codes)
        mine_a.append(send(next_a, ring_z))
        mine_b.append(send(next_b, ring_z))
        swap_a = mine_a[k] if k <= NEAR else after(mine_a[k], split[k - 1][0])
        their_a.append(send(swap_a, other_core))
        their_b.append(send(mine_b[k], other_core))
        if k <= NEAR:
            split.append(split_rows(where, mine_a[k], mine_b[k], their_a[k], their_b[k]))
    split = [part for pair in split for part in pair]

    pieces = chunk_products(
        1, where, codes, split, [mine_a[4], mine_b[4], their_a[4], their_b[4]]
    )
    wide, arrived = reduce_plane(pieces)
    far_home = bring_home(1, wide)
    pieces = chunk_products(0, where, after(codes, pieces[0]), split, [])
    near, _ = reduce_plane(pieces, arrived)
    near_home = bring_home(0, near)

    same, cross = [jnp.where(core == xhi, a, b) for a, b in zip(near_home, far_home)]
    first = jnp.where(core == 0, same, cross)
    second = jnp.where(core == 0, cross, same)
    return jnp.concatenate([first, second], axis=0)


def solution(mesh):
    fine = Mesh(mesh.devices.reshape(16, 2, 2, 2, 4), AXES)
    return jax.shard_map(
        shards,
        mesh=fine,
        in_specs=(P(AXES, None, None), P(AXES, None), P(("z", "xhi", "core"), None)),
        out_specs=P(AXES, None, None),
        check_vma=False,
    )
```

```python
import functools

import jax
import jax.numpy as jnp
from jax import lax
from jax.experimental import pallas as pl
from jax.experimental.pallas import tpu as pltpu
from jax.sharding import Mesh
from jax.sharding import PartitionSpec as P

NB = 1536
NZ = 16
AXES = ("z", "xhi", "core", "xlo", "y")
LEFT = (0, -4, 4, 0)
RIGHT = (0, 0, -4, -4)


def flat(z, xhi, core, xlo, y):
    return (((z % NZ * 2 + xhi) * 2 + core) * 2 + xlo) * 4 + y


def coords():
    for z in range(NZ):
        for xhi in range(2):
            for core in range(2):
                for xlo in range(2):
                    for y in range(4):
                        yield z, xhi, core, xlo, y


def send(value, target):
    pairs = []
    for at in coords():
        to = target(*at)
        if to is not None:
            pairs.append((flat(*at), flat(*to)))
    return lax.ppermute(value, AXES, pairs)


def other_core(z, xhi, core, xlo, y):
    return z, xhi, 1 - core, xlo, y


def ring_z(z, xhi, core, xlo, y):
    return (z - 1 if core == 0 else z + 1), xhi, core, xlo, y


def plane_step(phase, offset):
    def target(z, xhi, core, xlo, y):
        if phase == core:
            return z, xhi, core, xlo, (y + offset) % 4
        x = (xhi * 2 + xlo + offset) % 4
        return z, x // 2, core, x % 2, y

    return target


def home(chunk, same):
    def target(z, xhi, core, xlo, y):
        c = ((0, 3), (1, 2))[chunk][xhi]
        if (core == c % 2) != same:
            return None
        return z + LEFT[c], xhi, c % 2, xlo, y

    return target


def sort_kernel(ids_ref, blocks_ref, out_ref):
    count = blocks_ref.shape[0]
    keys = []
    for s in range(count):
        row = ids_ref[0, s]
        keys.append(jnp.where(row >= 0, row * NB + ids_ref[1, s], 2**30 + s))
    for s in range(count):
        rank = jnp.int32(0)
        for o in range(count):
            if o != s:
                rank = rank + jnp.where(keys[o] < keys[s], 1, 0)
        out_ref[rank] = blocks_ref[s]


def sort_blocks(block_ids, blocks):
    return pl.pallas_call(
        sort_kernel,
        out_shape=jax.ShapeDtypeStruct(blocks.shape, blocks.dtype),
        in_specs=[
            pl.BlockSpec(memory_space=pltpu.SMEM),
            pl.BlockSpec(memory_space=pltpu.VMEM),
        ],
        out_specs=pl.BlockSpec(memory_space=pltpu.VMEM),
        name="sort_blocks",
    )(block_ids.T, blocks)


REACH = 4


def split_into(panel, at, quarter, hi_ref, lo_ref):
    for rho in range(4):
        for col in range(2):
            x = panel[2 * rho + col]
            hi = x.astype(jnp.bfloat16)
            lo = (x - hi.astype(jnp.float32)).astype(jnp.bfloat16)
            lanes = pl.ds(pl.multiple_of(quarter * 256 + col * 128, 128), 128)
            hi_ref[at, rho * 128 : (rho + 1) * 128, lanes] = hi
            lo_ref[at, rho * 128 : (rho + 1) * 128, lanes] = lo


def split_pair(core, panels, hi_ref, lo_ref):
    ahead = 1 - core
    places = ((ahead, core), (ahead, 1 - core), (1 - ahead, 1 - core), (1 - ahead, core))
    for panel, (at, quarter) in zip(panels, places):
        split_into(panel, at, quarter, hi_ref, lo_ref)


def split_kernel(where_ref, *refs):
    core = where_ref[0]
    *panels, hi_ref, lo_ref = refs
    if len(panels) == 2:
        split_into(panels[0], 0, core, hi_ref, lo_ref)
        split_into(panels[1], 0, 1 - core, hi_ref, lo_ref)
    else:
        split_pair(core, panels, hi_ref, lo_ref)


def split_rows(where, *panels):
    vmem = pl.BlockSpec(memory_space=pltpu.VMEM)
    smem = pl.BlockSpec(memory_space=pltpu.SMEM)
    return pl.pallas_call(
        split_kernel,
        out_shape=[jax.ShapeDtypeStruct((len(panels) // 2, 512, 512), jnp.bfloat16)] * 2,
        in_specs=[smem] + [vmem] * len(panels),
        out_specs=[vmem] * 2,
        compiler_params=pltpu.CompilerParams(vmem_limit_bytes=8 << 20),
        name=f"split_{len(panels)}",
    )(where, *panels)


def chunk_kernel(chunk, where_ref, codes_ref, *refs):
    core = where_ref[0]
    place = where_ref[1]
    xhi = place // 8
    count = 2 * REACH + 2
    rows_hi, rows_lo = refs[:count:2], refs[1:count:2]
    outs = refs[count : count + 4]
    [res_ref] = refs[count + 4 :]

    def row(offset):
        at = int(offset > 0)
        return rows_hi[abs(offset)].at[at], rows_lo[abs(offset)].at[at]

    def times(a, b):
        return lax.dot_general(
            a[...], b[...], (((1,), (1,)), ((), ())), preferred_element_type=jnp.float32
        )

    lists = ((0, 3), (1, 2))[chunk]
    held = [(c % 2 ^ core) + 2 * (c // 2 ^ xhi) for c in lists]
    for far, c in enumerate(lists):
        left_hi, left_lo = row(LEFT[c])
        for step in range(4):
            right_hi, right_lo = row(RIGHT[c] + step)
            res_ref[far * 4 + step] = (
                times(left_hi, right_hi) + times(left_hi, right_lo) + times(left_lo, right_hi)
            )
    x, y = place // 4, place % 4
    for offset in range(4):

        def pick(index, carry, offset=offset):
            after_that = index // 4
            to_x = (x + jnp.where(core == 0, after_that, offset)) % 4
            to_y = (y + jnp.where(core == 0, offset, after_that)) % 4
            far = to_x // 2
            slot = (to_x % 2 * 4 + to_y) * 8 + core * 4 + index % 4
            code = codes_ref[jnp.where(far == 0, held[0], held[1]), slot]
            good = code >= 0
            code = jnp.maximum(code, 0)
            rows = pl.ds(pl.multiple_of(code // 16 * 128, 128), 128)
            cols = pl.ds(pl.multiple_of(code % 4 * 128, 128), 128)
            block = res_ref[far * 4 + code // 4 % 4, rows, cols]
            outs[offset][index] = jnp.where(good, block, jnp.float32(0.0))
            return carry

        lax.fori_loop(0, 16, pick, 0, unroll=4)


def chunk_products(chunk, where, codes, split):
    vmem = pl.BlockSpec(memory_space=pltpu.VMEM)
    smem = pl.BlockSpec(memory_space=pltpu.SMEM)
    return pl.pallas_call(
        functools.partial(chunk_kernel, chunk),
        out_shape=[jax.ShapeDtypeStruct((16, 128, 128), jnp.float32)] * 4,
        in_specs=[smem] * 2 + [vmem] * len(split),
        out_specs=[vmem] * 4,
        scratch_shapes=[pltpu.VMEM((8, 512, 512), jnp.float32)],
        compiler_params=pltpu.CompilerParams(vmem_limit_bytes=20 << 20),
        name=f"products_{chunk}",
    )(where, codes, *split)


def slot_codes(out_ids, row, col):
    i = out_ids[:, 0]
    j = out_ids[:, 1]
    good = (i >= 0) & (j >= 0)
    same_j = (j[None, :] == j[:, None]) & good[None, :]
    same_i = (i[None, :] == i[:, None]) & good[None, :]
    group = lax.rem(j, NZ)
    left = jnp.sum((same_j & (i[None, :] < i[:, None])).astype(jnp.int32), axis=1)
    right = jnp.sum(
        (same_i & (group[None, :] == group[:, None]) & (j[None, :] < j[:, None])).astype(jnp.int32),
        axis=1,
    )
    step = lax.rem(group - row - 4 * col + 8 * NZ, NZ)
    return jnp.where(good, left * 16 + step * 4 + right, -1)


def after(value, *others):
    return lax.optimization_barrier((value, *others))[0]


def reduce_plane(pieces, others=(), late=()):
    received = [None] * 4
    for offset in (2, 1, 3):
        received[offset] = send(pieces[offset], plane_step(0, offset))
    if others:
        received[1:] = lax.optimization_barrier((*others, *received[1:]))[-3:]
    count = pieces[0].shape[0] // 4
    total = [
        sum((received[o][n * count : (n + 1) * count] for o in (1, 2, 3)), pieces[0][n * count : (n + 1) * count])
        for n in range(4)
    ]
    arrived = [send(total[offset], plane_step(1, offset)) for offset in (2, 1, 3)]
    if late:
        arrived = lax.optimization_barrier((*late, *arrived))[-3:]
    return total[0] + arrived[0] + arrived[1] + arrived[2], arrived


def bring_home(part):
    return send(part, home(1, True)), send(part, home(1, False))


def to_place(z, xhi, core, xlo, y):
    return z - LEFT[xhi * 2 + core], xhi, core, xlo, y


def other_xhi(z, xhi, core, xlo, y):
    return z, 1 - xhi, core, xlo, y


def shards(blocks, block_ids, out_ids):
    z = lax.axis_index("z")
    xhi = lax.axis_index("xhi")
    core = lax.axis_index("core")
    x = xhi * 2 + lax.axis_index("xlo")
    where = jnp.stack([core, x * 4 + lax.axis_index("y")]).astype(jnp.int32)

    placed = send(out_ids, to_place)
    col = xhi * 2 + core
    left = jnp.where(col == 1, LEFT[1], jnp.where(col == 2, LEFT[2], LEFT[0]))
    codes = slot_codes(placed, z + left, col)[None]
    codes = jnp.concatenate([codes, send(codes, other_core)], axis=0)
    codes = jnp.concatenate([codes, send(codes, other_xhi)], axis=0)

    mine_a = [sort_blocks(block_ids, blocks)]
    mine_b = [send(mine_a[0], other_core)]
    split = [split_rows(where, mine_a[0], mine_b[0])]
    their_a, their_b = [None], [None]
    for k in range(1, REACH + 1):
        next_a, next_b = mine_a[-1], mine_b[-1]
        if k == 1:
            next_a = after(next_a, placed)
        if k > 2:
            next_a = after(next_a, their_a[k - 2])
            next_b = after(next_b, split[k - 2][0])
        mine_a.append(send(next_a, ring_z))
        mine_b.append(send(next_b, ring_z))
        swap_a = mine_a[k] if k < REACH else after(mine_a[k], split[k - 1][0], codes)
        their_a.append(send(swap_a, other_core))
        their_b.append(send(mine_b[k], other_core))
        split.append(split_rows(where, mine_a[k], mine_b[k], their_a[k], their_b[k]))
    split = [part for pair in split for part in pair]

    pieces = chunk_products(1, where, codes, split)
    wide, arrived = reduce_plane(pieces)
    far_same, far_cross = bring_home(wide)
    pieces = chunk_products(0, where, after(codes, pieces[0]), split)
    near, _ = reduce_plane(pieces, [wide], (far_same, far_cross))
    near_cross = send(near, home(0, False))

    same = jnp.where(core == xhi, near, far_same)
    cross = jnp.where(core == xhi, near_cross, far_cross)
    first = jnp.where(core == 0, same, cross)
    second = jnp.where(core == 0, cross, same)
    return jnp.concatenate([first, second], axis=0)


def solution(mesh):
    fine = Mesh(mesh.devices.reshape(16, 2, 2, 2, 4), AXES)
    return jax.shard_map(
        shards,
        mesh=fine,
        in_specs=(P(AXES, None, None), P(AXES, None), P(("z", "xhi", "core"), None)),
        out_specs=P(AXES, None, None),
        check_vma=False,
    )
```

```python
import functools

import jax
import jax.numpy as jnp
from jax import lax
from jax.experimental import pallas as pl
from jax.experimental.pallas import tpu as pltpu
from jax.sharding import Mesh
from jax.sharding import PartitionSpec as P

NB = 1536
NZ = 16
AXES = ("z", "xhi", "core", "xlo", "y")
LEFT = (0, -4, 4, 0)
RIGHT = (0, 0, -4, -4)


def flat(z, xhi, core, xlo, y):
    return (((z % NZ * 2 + xhi) * 2 + core) * 2 + xlo) * 4 + y


def coords():
    for z in range(NZ):
        for xhi in range(2):
            for core in range(2):
                for xlo in range(2):
                    for y in range(4):
                        yield z, xhi, core, xlo, y


def send(value, target):
    pairs = []
    for at in coords():
        to = target(*at)
        if to is not None:
            pairs.append((flat(*at), flat(*to)))
    return lax.ppermute(value, AXES, pairs)


def other_core(z, xhi, core, xlo, y):
    return z, xhi, 1 - core, xlo, y


def ring_z(z, xhi, core, xlo, y):
    return (z - 1 if core == 0 else z + 1), xhi, core, xlo, y


def plane_step(phase, offset):
    def target(z, xhi, core, xlo, y):
        if phase == core:
            return z, xhi, core, xlo, (y + offset) % 4
        x = (xhi * 2 + xlo + offset) % 4
        return z, x // 2, core, x % 2, y

    return target


def home(chunk, same):
    def target(z, xhi, core, xlo, y):
        c = ((0, 3), (1, 2))[chunk][xhi]
        if (core == c % 2) != same:
            return None
        return z + LEFT[c], xhi, c % 2, xlo, y

    return target


def sort_kernel(ids_ref, blocks_ref, out_ref):
    count = blocks_ref.shape[0]
    keys = []
    for s in range(count):
        row = ids_ref[0, s]
        keys.append(jnp.where(row >= 0, row * NB + ids_ref[1, s], 2**30 + s))
    for s in range(count):
        rank = jnp.int32(0)
        for o in range(count):
            if o != s:
                rank = rank + jnp.where(keys[o] < keys[s], 1, 0)
        out_ref[rank] = blocks_ref[s]


def sort_blocks(block_ids, blocks):
    return pl.pallas_call(
        sort_kernel,
        out_shape=jax.ShapeDtypeStruct(blocks.shape, blocks.dtype),
        in_specs=[
            pl.BlockSpec(memory_space=pltpu.SMEM),
            pl.BlockSpec(memory_space=pltpu.VMEM),
        ],
        out_specs=pl.BlockSpec(memory_space=pltpu.VMEM),
        name="sort_blocks",
    )(block_ids.T, blocks)


REACH = 4


def split_into(panel, at, quarter, hi_ref, lo_ref):
    for rho in range(4):
        for col in range(2):
            x = panel[2 * rho + col]
            hi = x.astype(jnp.bfloat16)
            lo = (x - hi.astype(jnp.float32)).astype(jnp.bfloat16)
            lanes = pl.ds(pl.multiple_of(quarter * 256 + col * 128, 128), 128)
            hi_ref[at, rho * 128 : (rho + 1) * 128, lanes] = hi
            lo_ref[at, rho * 128 : (rho + 1) * 128, lanes] = lo


def split_pair(core, panels, hi_ref, lo_ref):
    ahead = 1 - core
    places = ((ahead, core), (ahead, 1 - core), (1 - ahead, 1 - core), (1 - ahead, core))
    for panel, (at, quarter) in zip(panels, places):
        split_into(panel, at, quarter, hi_ref, lo_ref)


def split_kernel(where_ref, *refs):
    core = where_ref[0]
    *panels, hi_ref, lo_ref = refs
    if len(panels) == 2:
        split_into(panels[0], 0, core, hi_ref, lo_ref)
        split_into(panels[1], 0, 1 - core, hi_ref, lo_ref)
    else:
        split_pair(core, panels, hi_ref, lo_ref)


def split_rows(where, *panels):
    vmem = pl.BlockSpec(memory_space=pltpu.VMEM)
    smem = pl.BlockSpec(memory_space=pltpu.SMEM)
    return pl.pallas_call(
        split_kernel,
        out_shape=[jax.ShapeDtypeStruct((len(panels) // 2, 512, 512), jnp.bfloat16)] * 2,
        in_specs=[smem] + [vmem] * len(panels),
        out_specs=[vmem] * 2,
        compiler_params=pltpu.CompilerParams(vmem_limit_bytes=8 << 20),
        name=f"split_{len(panels)}",
    )(where, *panels)


def chunk_kernel(chunk, where_ref, codes_ref, *refs):
    core = where_ref[0]
    place = where_ref[1]
    xhi = place // 8
    count = 2 * REACH + 2
    rows_hi, rows_lo = refs[:count:2], refs[1:count:2]
    outs = refs[count : count + 4]
    [res_ref] = refs[count + 4 :]

    def row(offset):
        at = int(offset > 0)
        return rows_hi[abs(offset)].at[at], rows_lo[abs(offset)].at[at]

    def times(a, b):
        return lax.dot_general(
            a[...], b[...], (((1,), (1,)), ((), ())), preferred_element_type=jnp.float32
        )

    lists = ((0, 3), (1, 2))[chunk]
    held = [(c % 2 ^ core) + 2 * (c // 2 ^ xhi) for c in lists]
    for far, c in enumerate(lists):
        left_hi, left_lo = row(LEFT[c])
        for step in range(4):
            right_hi, right_lo = row(RIGHT[c] + step)
            res_ref[far * 4 + step] = (
                times(left_hi, right_hi) + times(left_hi, right_lo) + times(left_lo, right_hi)
            )
    x, y = place // 4, place % 4
    for offset in range(4):

        def pick(index, carry, offset=offset):
            after_that = index // 4
            to_x = (x + jnp.where(core == 0, after_that, offset)) % 4
            to_y = (y + jnp.where(core == 0, offset, after_that)) % 4
            far = to_x // 2
            slot = (to_x % 2 * 4 + to_y) * 8 + core * 4 + index % 4
            code = codes_ref[jnp.where(far == 0, held[0], held[1]), slot]
            good = code >= 0
            code = jnp.maximum(code, 0)
            rows = pl.ds(pl.multiple_of(code // 16 * 128, 128), 128)
            cols = pl.ds(pl.multiple_of(code % 4 * 128, 128), 128)
            block = res_ref[far * 4 + code // 4 % 4, rows, cols]
            outs[offset][index] = jnp.where(good, block, jnp.float32(0.0))
            return carry

        lax.fori_loop(0, 16, pick, 0, unroll=4)


def chunk_products(chunk, where, codes, split):
    vmem = pl.BlockSpec(memory_space=pltpu.VMEM)
    smem = pl.BlockSpec(memory_space=pltpu.SMEM)
    return pl.pallas_call(
        functools.partial(chunk_kernel, chunk),
        out_shape=[jax.ShapeDtypeStruct((16, 128, 128), jnp.float32)] * 4,
        in_specs=[smem] * 2 + [vmem] * len(split),
        out_specs=[vmem] * 4,
        scratch_shapes=[pltpu.VMEM((8, 512, 512), jnp.float32)],
        compiler_params=pltpu.CompilerParams(vmem_limit_bytes=20 << 20),
        name=f"products_{chunk}",
    )(where, codes, *split)


def slot_codes(out_ids, row, col):
    i = out_ids[:, 0]
    j = out_ids[:, 1]
    good = (i >= 0) & (j >= 0)
    same_j = (j[None, :] == j[:, None]) & good[None, :]
    same_i = (i[None, :] == i[:, None]) & good[None, :]
    group = lax.rem(j, NZ)
    left = jnp.sum((same_j & (i[None, :] < i[:, None])).astype(jnp.int32), axis=1)
    right = jnp.sum(
        (same_i & (group[None, :] == group[:, None]) & (j[None, :] < j[:, None])).astype(jnp.int32),
        axis=1,
    )
    step = lax.rem(group - row - 4 * col + 8 * NZ, NZ)
    return jnp.where(good, left * 16 + step * 4 + right, -1)


def after(value, *others):
    return lax.optimization_barrier((value, *others))[0]


def reduce_plane(pieces, others=(), late=(), third=()):
    received = [None] * 4
    for offset in (2, 1, 3):
        piece = pieces[offset]
        if third and offset == 3:
            piece = after(piece, *third)
        received[offset] = send(piece, plane_step(0, offset))
    if others:
        received[1:] = lax.optimization_barrier((*others, *received[1:]))[-3:]
    count = pieces[0].shape[0] // 4
    total = [
        sum((received[o][n * count : (n + 1) * count] for o in (1, 2, 3)), pieces[0][n * count : (n + 1) * count])
        for n in range(4)
    ]
    arrived = [send(total[offset], plane_step(1, offset)) for offset in (2, 1, 3)]
    if late:
        arrived = lax.optimization_barrier((*late, *arrived))[-3:]
    return total[0] + arrived[0] + arrived[1] + arrived[2], arrived


def bring_home(part):
    return send(part, home(1, True)), send(part, home(1, False))


def to_place(z, xhi, core, xlo, y):
    return z - LEFT[xhi * 2 + core], xhi, core, xlo, y


def other_xhi(z, xhi, core, xlo, y):
    return z, 1 - xhi, core, xlo, y


def shards(blocks, block_ids, out_ids):
    z = lax.axis_index("z")
    xhi = lax.axis_index("xhi")
    core = lax.axis_index("core")
    x = xhi * 2 + lax.axis_index("xlo")
    where = jnp.stack([core, x * 4 + lax.axis_index("y")]).astype(jnp.int32)

    placed = send(out_ids, to_place)
    col = xhi * 2 + core
    left = jnp.where(col == 1, LEFT[1], jnp.where(col == 2, LEFT[2], 0))
    codes = slot_codes(placed, z + left, col)[None]
    chip_codes = jnp.concatenate([codes, send(codes, other_core)], axis=0)
    codes = jnp.concatenate([chip_codes, send(chip_codes, other_xhi)], axis=0)

    mine_a = [sort_blocks(block_ids, blocks)]
    mine_b = [send(mine_a[0], other_core)]
    split = [split_rows(where, mine_a[0], mine_b[0])]
    their_a, their_b = [None], [None]
    for k in range(1, REACH + 1):
        next_a, next_b = mine_a[-1], mine_b[-1]
        if k == 1:
            next_b = after(next_b, placed)
        if k == 2:
            next_b = after(next_b, chip_codes)
        if k == 3:
            next_b = after(next_b, codes)
        if k > 2:
            next_a = after(next_a, their_a[k - 2])
            next_b = after(next_b, split[k - 2][0])
        mine_a.append(send(next_a, ring_z))
        mine_b.append(send(next_b, ring_z))
        swap_a = mine_a[k] if k < REACH else after(mine_a[k], split[k - 1][0])
        their_a.append(send(swap_a, other_core))
        their_b.append(send(mine_b[k], other_core))
        split.append(split_rows(where, mine_a[k], mine_b[k], their_a[k], their_b[k]))
    split = [part for pair in split for part in pair]

    pieces = chunk_products(1, where, codes, split)
    wide, arrived = reduce_plane(pieces)
    far_same, far_cross = bring_home(wide)
    pieces = chunk_products(0, where, after(codes, pieces[0]), split)
    near, _ = reduce_plane(pieces, [wide], (far_same, far_cross), ())
    near_cross = send(near, home(0, False))

    same = jnp.where(core == xhi, near, far_same)
    cross = jnp.where(core == xhi, near_cross, far_cross)
    first = jnp.where(core == 0, same, cross)
    second = jnp.where(core == 0, cross, same)
    return jnp.concatenate([first, second], axis=0)


def solution(mesh):
    fine = Mesh(mesh.devices.reshape(16, 2, 2, 2, 4), AXES)
    return jax.shard_map(
        shards,
        mesh=fine,
        in_specs=(P(AXES, None, None), P(AXES, None), P(("z", "xhi", "core"), None)),
        out_specs=P(AXES, None, None),
        check_vma=False,
    )
```

```python
import functools

import jax
import jax.numpy as jnp
from jax import lax
from jax.experimental import pallas as pl
from jax.experimental.pallas import tpu as pltpu
from jax.sharding import Mesh
from jax.sharding import PartitionSpec as P

NB = 1536
NZ = 16
AXES = ("z", "xhi", "core", "xlo", "y")
LEFT = (0, -4, 4, 0)
RIGHT = (0, 0, -4, -4)


def flat(z, xhi, core, xlo, y):
    return (((z % NZ * 2 + xhi) * 2 + core) * 2 + xlo) * 4 + y


def coords():
    for z in range(NZ):
        for xhi in range(2):
            for core in range(2):
                for xlo in range(2):
                    for y in range(4):
                        yield z, xhi, core, xlo, y


def send(value, target):
    pairs = []
    for at in coords():
        to = target(*at)
        if to is not None:
            pairs.append((flat(*at), flat(*to)))
    return lax.ppermute(value, AXES, pairs)


def other_core(z, xhi, core, xlo, y):
    return z, xhi, 1 - core, xlo, y


def ring_z(z, xhi, core, xlo, y):
    return (z - 1 if core == 0 else z + 1), xhi, core, xlo, y


def plane_step(phase, offset):
    def target(z, xhi, core, xlo, y):
        if phase == core:
            return z, xhi, core, xlo, (y + offset) % 4
        x = (xhi * 2 + xlo + offset) % 4
        return z, x // 2, core, x % 2, y

    return target


def home(chunk, same):
    def target(z, xhi, core, xlo, y):
        c = ((0, 3), (1, 2))[chunk][xhi]
        if (core == c % 2) != same:
            return None
        return z + LEFT[c], xhi, c % 2, xlo, y

    return target


def sort_kernel(ids_ref, blocks_ref, out_ref):
    count = blocks_ref.shape[0]
    keys = []
    for s in range(count):
        row = ids_ref[0, s]
        keys.append(jnp.where(row >= 0, row * NB + ids_ref[1, s], 2**30 + s))
    for s in range(count):
        rank = jnp.int32(0)
        for o in range(count):
            if o != s:
                rank = rank + jnp.where(keys[o] < keys[s], 1, 0)
        out_ref[rank] = blocks_ref[s]


def sort_blocks(block_ids, blocks):
    return pl.pallas_call(
        sort_kernel,
        out_shape=jax.ShapeDtypeStruct(blocks.shape, blocks.dtype),
        in_specs=[
            pl.BlockSpec(memory_space=pltpu.SMEM),
            pl.BlockSpec(memory_space=pltpu.VMEM),
        ],
        out_specs=pl.BlockSpec(memory_space=pltpu.VMEM),
        name="sort_blocks",
    )(block_ids.T, blocks)


REACH = 4


def split_into(panel, at, quarter, hi_ref, lo_ref):
    for rho in range(4):
        for col in range(2):
            x = panel[2 * rho + col]
            hi = x.astype(jnp.bfloat16)
            lo = (x - hi.astype(jnp.float32)).astype(jnp.bfloat16)
            lanes = pl.ds(pl.multiple_of(quarter * 256 + col * 128, 128), 128)
            hi_ref[at, rho * 128 : (rho + 1) * 128, lanes] = hi
            lo_ref[at, rho * 128 : (rho + 1) * 128, lanes] = lo


def split_pair(core, panels, hi_ref, lo_ref):
    ahead = 1 - core
    places = ((ahead, core), (ahead, 1 - core), (1 - ahead, 1 - core), (1 - ahead, core))
    for panel, (at, quarter) in zip(panels, places):
        split_into(panel, at, quarter, hi_ref, lo_ref)


def split_kernel(where_ref, *refs):
    core = where_ref[0]
    *panels, hi_ref, lo_ref = refs
    if len(panels) == 2:
        split_into(panels[0], 0, core, hi_ref, lo_ref)
        split_into(panels[1], 0, 1 - core, hi_ref, lo_ref)
    else:
        split_pair(core, panels, hi_ref, lo_ref)


def split_rows(where, *panels):
    vmem = pl.BlockSpec(memory_space=pltpu.VMEM)
    smem = pl.BlockSpec(memory_space=pltpu.SMEM)
    return pl.pallas_call(
        split_kernel,
        out_shape=[jax.ShapeDtypeStruct((len(panels) // 2, 512, 512), jnp.bfloat16)] * 2,
        in_specs=[smem] + [vmem] * len(panels),
        out_specs=[vmem] * 2,
        compiler_params=pltpu.CompilerParams(vmem_limit_bytes=8 << 20),
        name=f"split_{len(panels)}",
    )(where, *panels)


def chunk_kernel(chunk, where_ref, codes_ref, *refs):
    core = where_ref[0]
    place = where_ref[1]
    xhi = place // 8
    count = 2 * REACH + 2
    rows_hi, rows_lo = refs[:count:2], refs[1:count:2]
    outs = refs[count : count + 4]
    [res_ref] = refs[count + 4 :]

    def row(offset):
        at = int(offset > 0)
        return rows_hi[abs(offset)].at[at], rows_lo[abs(offset)].at[at]

    def times(a, b):
        return lax.dot_general(
            a[...], b[...], (((1,), (1,)), ((), ())), preferred_element_type=jnp.float32
        )

    lists = ((0, 3), (1, 2))[chunk]
    held = [(c % 2 ^ core) + 2 * (c // 2 ^ xhi) for c in lists]
    for far, c in enumerate(lists):
        left_hi, left_lo = row(LEFT[c])
        for step in range(4):
            right_hi, right_lo = row(RIGHT[c] + step)
            res_ref[far * 4 + step] = (
                times(left_hi, right_hi) + times(left_hi, right_lo) + times(left_lo, right_hi)
            )
    x, y = place // 4, place % 4
    for offset in range(4):

        def pick(index, carry, offset=offset):
            after_that = index // 4
            to_x = (x + jnp.where(core == 0, after_that, offset)) % 4
            to_y = (y + jnp.where(core == 0, offset, after_that)) % 4
            far = to_x // 2
            slot = (to_x % 2 * 4 + to_y) * 8 + core * 4 + index % 4
            code = codes_ref[jnp.where(far == 0, held[0], held[1]), slot]
            good = code >= 0
            code = jnp.maximum(code, 0)
            rows = pl.ds(pl.multiple_of(code // 16 * 128, 128), 128)
            cols = pl.ds(pl.multiple_of(code % 4 * 128, 128), 128)
            block = res_ref[far * 4 + code // 4 % 4, rows, cols]
            outs[offset][index] = jnp.where(good, block, jnp.float32(0.0))
            return carry

        lax.fori_loop(0, 16, pick, 0, unroll=4)


def chunk_products(chunk, where, codes, split):
    vmem = pl.BlockSpec(memory_space=pltpu.VMEM)
    smem = pl.BlockSpec(memory_space=pltpu.SMEM)
    return pl.pallas_call(
        functools.partial(chunk_kernel, chunk),
        out_shape=[jax.ShapeDtypeStruct((16, 128, 128), jnp.float32)] * 4,
        in_specs=[smem] * 2 + [vmem] * len(split),
        out_specs=[vmem] * 4,
        scratch_shapes=[pltpu.VMEM((8, 512, 512), jnp.float32)],
        compiler_params=pltpu.CompilerParams(vmem_limit_bytes=20 << 20),
        name=f"products_{chunk}",
    )(where, codes, *split)


def slot_codes(out_ids, row, col):
    i = out_ids[:, 0]
    j = out_ids[:, 1]
    good = (i >= 0) & (j >= 0)
    same_j = (j[None, :] == j[:, None]) & good[None, :]
    same_i = (i[None, :] == i[:, None]) & good[None, :]
    group = lax.rem(j, NZ)
    left = jnp.sum((same_j & (i[None, :] < i[:, None])).astype(jnp.int32), axis=1)
    right = jnp.sum(
        (same_i & (group[None, :] == group[:, None]) & (j[None, :] < j[:, None])).astype(jnp.int32),
        axis=1,
    )
    step = lax.rem(group - row - 4 * col + 8 * NZ, NZ)
    return jnp.where(good, left * 16 + step * 4 + right, -1)


def after(value, *others):
    return lax.optimization_barrier((value, *others))[0]


def reduce_plane(pieces, others=(), late=(), third=()):
    received = [None] * 4
    for offset in (2, 1, 3):
        piece = pieces[offset]
        if third and offset == 3:
            piece = after(piece, *third)
        received[offset] = send(piece, plane_step(0, offset))
    if others:
        received[1:] = lax.optimization_barrier((*others, *received[1:]))[-3:]
    count = pieces[0].shape[0] // 4
    total = [
        sum((received[o][n * count : (n + 1) * count] for o in (1, 2, 3)), pieces[0][n * count : (n + 1) * count])
        for n in range(4)
    ]
    arrived = [send(total[offset], plane_step(1, offset)) for offset in (2, 1, 3)]
    if late:
        arrived = lax.optimization_barrier((*late, *arrived))[-3:]
    return total[0] + arrived[0] + arrived[1] + arrived[2], arrived


def bring_home(part):
    return send(part, home(1, True)), send(part, home(1, False))


def to_place(z, xhi, core, xlo, y):
    return z - LEFT[xhi * 2 + core], xhi, core, xlo, y


def other_xhi(z, xhi, core, xlo, y):
    return z, 1 - xhi, core, xlo, y


def shards(blocks, block_ids, out_ids):
    z = lax.axis_index("z")
    xhi = lax.axis_index("xhi")
    core = lax.axis_index("core")
    x = xhi * 2 + lax.axis_index("xlo")
    where = jnp.stack([core, x * 4 + lax.axis_index("y")]).astype(jnp.int32)

    placed = send(out_ids, to_place)
    col = xhi * 2 + core
    left = jnp.where(col == 1, LEFT[1], jnp.where(col == 2, LEFT[2], 0))
    codes = slot_codes(placed, z + left, col)[None]
    chip_codes = jnp.concatenate([codes, send(codes, other_core)], axis=0)
    codes = jnp.concatenate([chip_codes, send(chip_codes, other_xhi)], axis=0)

    mine_a = [sort_blocks(block_ids, blocks)]
    mine_b = [send(mine_a[0], other_core)]
    split = [split_rows(where, mine_a[0], mine_b[0])]
    their_a, their_b = [None], [None]
    for k in range(1, REACH + 1):
        next_a, next_b = mine_a[-1], mine_b[-1]
        if k == 1:
            next_b = after(next_b, placed)
        if k == 2:
            next_b = after(next_b, chip_codes)
        if k == 3:
            next_b = after(next_b, codes)
        if k > 2:
            next_a = after(next_a, their_a[k - 2])
            next_b = after(next_b, split[k - 2][0])
        mine_a.append(send(next_a, ring_z))
        mine_b.append(send(next_b, ring_z))
        swap_a = mine_a[k] if k < REACH else mine_a[k]
        their_a.append(send(swap_a, other_core))
        their_b.append(send(mine_b[k], other_core))
        split.append(split_rows(where, mine_a[k], mine_b[k], their_a[k], their_b[k]))
    split = [part for pair in split for part in pair]

    pieces = chunk_products(1, where, codes, split)
    wide, arrived = reduce_plane(pieces)
    far_same, far_cross = bring_home(wide)
    pieces = chunk_products(0, where, after(codes, pieces[0]), split)
    near, _ = reduce_plane(pieces, [wide], (far_same, far_cross), ())
    near_cross = send(near, home(0, False))

    same = jnp.where(core == xhi, near, far_same)
    cross = jnp.where(core == xhi, near_cross, far_cross)
    first = jnp.where(core == 0, same, cross)
    second = jnp.where(core == 0, cross, same)
    return jnp.concatenate([first, second], axis=0)


def solution(mesh):
    fine = Mesh(mesh.devices.reshape(16, 2, 2, 2, 4), AXES)
    return jax.shard_map(
        shards,
        mesh=fine,
        in_specs=(P(AXES, None, None), P(AXES, None), P(("z", "xhi", "core"), None)),
        out_specs=P(AXES, None, None),
        check_vma=False,
    )
```

```python
import functools

import jax
import jax.numpy as jnp
from jax import lax
from jax.experimental import pallas as pl
from jax.experimental.pallas import tpu as pltpu
from jax.sharding import Mesh
from jax.sharding import PartitionSpec as P

NB = 1536
NZ = 16
AXES = ("z", "xhi", "core", "xlo", "y")
LEFT = (0, -4, 4, 0)
RIGHT = (0, 0, -4, -4)


def flat(z, xhi, core, xlo, y):
    return (((z % NZ * 2 + xhi) * 2 + core) * 2 + xlo) * 4 + y


def coords():
    for z in range(NZ):
        for xhi in range(2):
            for core in range(2):
                for xlo in range(2):
                    for y in range(4):
                        yield z, xhi, core, xlo, y


def send(value, target):
    pairs = []
    for at in coords():
        to = target(*at)
        if to is not None:
            pairs.append((flat(*at), flat(*to)))
    return lax.ppermute(value, AXES, pairs)


def other_core(z, xhi, core, xlo, y):
    return z, xhi, 1 - core, xlo, y


def ring_z(z, xhi, core, xlo, y):
    return (z - 1 if core == 0 else z + 1), xhi, core, xlo, y


def plane_step(phase, offset):
    def target(z, xhi, core, xlo, y):
        if phase == core:
            return z, xhi, core, xlo, (y + offset) % 4
        x = (xhi * 2 + xlo + offset) % 4
        return z, x // 2, core, x % 2, y

    return target


def home(chunk, same):
    def target(z, xhi, core, xlo, y):
        c = ((0, 3), (1, 2))[chunk][xhi]
        if (core == c % 2) != same:
            return None
        return z + LEFT[c], xhi, c % 2, xlo, y

    return target


def sort_kernel(ids_ref, blocks_ref, out_ref):
    count = blocks_ref.shape[0]
    keys = []
    for s in range(count):
        row = ids_ref[0, s]
        keys.append(jnp.where(row >= 0, row * NB + ids_ref[1, s], 2**30 + s))
    for s in range(count):
        rank = jnp.int32(0)
        for o in range(count):
            if o != s:
                rank = rank + jnp.where(keys[o] < keys[s], 1, 0)
        out_ref[rank] = blocks_ref[s]


def sort_blocks(block_ids, blocks):
    return pl.pallas_call(
        sort_kernel,
        out_shape=jax.ShapeDtypeStruct(blocks.shape, blocks.dtype),
        in_specs=[
            pl.BlockSpec(memory_space=pltpu.SMEM),
            pl.BlockSpec(memory_space=pltpu.VMEM),
        ],
        out_specs=pl.BlockSpec(memory_space=pltpu.VMEM),
        name="sort_blocks",
    )(block_ids.T, blocks)


REACH = 4


def split_into(panel, at, quarter, hi_ref, lo_ref):
    for rho in range(4):
        for col in range(2):
            x = panel[2 * rho + col]
            hi = x.astype(jnp.bfloat16)
            lo = (x - hi.astype(jnp.float32)).astype(jnp.bfloat16)
            lanes = pl.ds(pl.multiple_of(quarter * 256 + col * 128, 128), 128)
            hi_ref[at, rho * 128 : (rho + 1) * 128, lanes] = hi
            lo_ref[at, rho * 128 : (rho + 1) * 128, lanes] = lo


def split_pair(core, panels, hi_ref, lo_ref):
    ahead = 1 - core
    places = ((ahead, core), (ahead, 1 - core), (1 - ahead, 1 - core), (1 - ahead, core))
    for panel, (at, quarter) in zip(panels, places):
        split_into(panel, at, quarter, hi_ref, lo_ref)


def split_kernel(where_ref, *refs):
    core = where_ref[0]
    *panels, hi_ref, lo_ref = refs
    if len(panels) == 2:
        split_into(panels[0], 0, core, hi_ref, lo_ref)
        split_into(panels[1], 0, 1 - core, hi_ref, lo_ref)
    else:
        split_pair(core, panels, hi_ref, lo_ref)


def split_rows(where, *panels):
    vmem = pl.BlockSpec(memory_space=pltpu.VMEM)
    smem = pl.BlockSpec(memory_space=pltpu.SMEM)
    return pl.pallas_call(
        split_kernel,
        out_shape=[jax.ShapeDtypeStruct((len(panels) // 2, 512, 512), jnp.bfloat16)] * 2,
        in_specs=[smem] + [vmem] * len(panels),
        out_specs=[vmem] * 2,
        compiler_params=pltpu.CompilerParams(vmem_limit_bytes=8 << 20),
        name=f"split_{len(panels)}",
    )(where, *panels)


def chunk_kernel(chunk, where_ref, codes_ref, *refs):
    core = where_ref[0]
    place = where_ref[1]
    xhi = place // 8
    count = 2 * REACH + 2
    rows_hi, rows_lo = refs[:count:2], refs[1:count:2]
    outs = refs[count : count + 4]
    [res_ref] = refs[count + 4 :]

    def row(offset):
        at = int(offset > 0)
        return rows_hi[abs(offset)].at[at], rows_lo[abs(offset)].at[at]

    def times(a, b):
        return lax.dot_general(
            a[...], b[...], (((1,), (1,)), ((), ())), preferred_element_type=jnp.float32
        )

    lists = ((0, 3), (1, 2))[chunk]
    held = [(c % 2 ^ core) + 2 * (c // 2 ^ xhi) for c in lists]
    for far, c in enumerate(lists):
        left_hi, left_lo = row(LEFT[c])
        for step in range(4):
            right_hi, right_lo = row(RIGHT[c] + step)
            res_ref[far * 4 + step] = (
                times(left_hi, right_hi) + times(left_hi, right_lo) + times(left_lo, right_hi)
            )
    x, y = place // 4, place % 4
    for offset in range(4):

        def pick(index, carry, offset=offset):
            after_that = index // 4
            to_x = (x + jnp.where(core == 0, after_that, offset)) % 4
            to_y = (y + jnp.where(core == 0, offset, after_that)) % 4
            far = to_x // 2
            slot = (to_x % 2 * 4 + to_y) * 8 + core * 4 + index % 4
            code = codes_ref[jnp.where(far == 0, held[0], held[1]), slot]
            good = code >= 0
            code = jnp.maximum(code, 0)
            rows = pl.ds(pl.multiple_of(code // 16 * 128, 128), 128)
            cols = pl.ds(pl.multiple_of(code % 4 * 128, 128), 128)
            block = res_ref[far * 4 + code // 4 % 4, rows, cols]
            outs[offset][index] = jnp.where(good, block, jnp.float32(0.0))
            return carry

        lax.fori_loop(0, 16, pick, 0, unroll=4)


def chunk_products(chunk, where, codes, split):
    vmem = pl.BlockSpec(memory_space=pltpu.VMEM)
    smem = pl.BlockSpec(memory_space=pltpu.SMEM)
    return pl.pallas_call(
        functools.partial(chunk_kernel, chunk),
        out_shape=[jax.ShapeDtypeStruct((16, 128, 128), jnp.float32)] * 4,
        in_specs=[smem] * 2 + [vmem] * len(split),
        out_specs=[vmem] * 4,
        scratch_shapes=[pltpu.VMEM((8, 512, 512), jnp.float32)],
        compiler_params=pltpu.CompilerParams(vmem_limit_bytes=20 << 20),
        name=f"products_{chunk}",
    )(where, codes, *split)


def slot_codes(out_ids, row, col):
    i = out_ids[:, 0]
    j = out_ids[:, 1]
    good = (i >= 0) & (j >= 0)
    same_j = (j[None, :] == j[:, None]) & good[None, :]
    same_i = (i[None, :] == i[:, None]) & good[None, :]
    group = lax.rem(j, NZ)
    left = jnp.sum((same_j & (i[None, :] < i[:, None])).astype(jnp.int32), axis=1)
    right = jnp.sum(
        (same_i & (group[None, :] == group[:, None]) & (j[None, :] < j[:, None])).astype(jnp.int32),
        axis=1,
    )
    step = lax.rem(group - row - 4 * col + 8 * NZ, NZ)
    return jnp.where(good, left * 16 + step * 4 + right, -1)


def after(value, *others):
    return lax.optimization_barrier((value, *others))[0]


def reduce_plane(pieces, others=(), late=(), third=()):
    received = [None] * 4
    for offset in (2, 1, 3):
        piece = pieces[offset]
        if third and offset == 3:
            piece = after(piece, *third)
        received[offset] = send(piece, plane_step(0, offset))
    if others:
        received[1:] = lax.optimization_barrier((*others, *received[1:]))[-3:]
    count = pieces[0].shape[0] // 4
    total = [
        sum((received[o][n * count : (n + 1) * count] for o in (1, 2, 3)), pieces[0][n * count : (n + 1) * count])
        for n in range(4)
    ]
    arrived = [send(total[offset], plane_step(1, offset)) for offset in (2, 1, 3)]
    if late:
        arrived = lax.optimization_barrier((*late, *arrived))[-3:]
    return total[0] + arrived[0] + arrived[1] + arrived[2], arrived


def bring_home(part):
    return send(part, home(1, True)), send(part, home(1, False))


def to_place(z, xhi, core, xlo, y):
    return z - LEFT[xhi * 2 + core], xhi, core, xlo, y


def other_xhi(z, xhi, core, xlo, y):
    return z, 1 - xhi, core, xlo, y


def shards(blocks, block_ids, out_ids):
    z = lax.axis_index("z")
    xhi = lax.axis_index("xhi")
    core = lax.axis_index("core")
    x = xhi * 2 + lax.axis_index("xlo")
    where = jnp.stack([core, x * 4 + lax.axis_index("y")]).astype(jnp.int32)

    placed = send(out_ids, to_place)
    col = xhi * 2 + core
    left = jnp.where(col == 1, LEFT[1], jnp.where(col == 2, LEFT[2], 0))
    codes = slot_codes(placed, z + left, col)[None]
    chip_codes = jnp.concatenate([codes, send(codes, other_core)], axis=0)
    codes = jnp.concatenate([chip_codes, send(chip_codes, other_xhi)], axis=0)

    mine_a = [sort_blocks(block_ids, blocks)]
    mine_b = [send(mine_a[0], other_core)]
    split = [split_rows(where, mine_a[0], mine_b[0])]
    their_a, their_b = [None], [None]
    for k in range(1, REACH + 1):
        next_a, next_b = mine_a[-1], mine_b[-1]
        if k == 2:
            next_b = after(next_b, placed)
        if k == 3:
            next_b = after(next_b, chip_codes)
        if k == 4:
            next_b = after(next_b, codes)
        if k > 2:
            next_a = after(next_a, their_a[k - 2])
            next_b = after(next_b, split[k - 2][0])
        mine_a.append(send(next_a, ring_z))
        mine_b.append(send(next_b, ring_z))
        swap_a = mine_a[k] if k < REACH else mine_a[k]
        their_a.append(send(swap_a, other_core))
        their_b.append(send(mine_b[k], other_core))
        split.append(split_rows(where, mine_a[k], mine_b[k], their_a[k], their_b[k]))
    split = [part for pair in split for part in pair]

    pieces = chunk_products(1, where, codes, split)
    wide, arrived = reduce_plane(pieces)
    far_same, far_cross = bring_home(wide)
    pieces = chunk_products(0, where, after(codes, pieces[0]), split)
    near, _ = reduce_plane(pieces, [wide], (far_same, far_cross), ())
    near_cross = send(near, home(0, False))

    same = jnp.where(core == xhi, near, far_same)
    cross = jnp.where(core == xhi, near_cross, far_cross)
    first = jnp.where(core == 0, same, cross)
    second = jnp.where(core == 0, cross, same)
    return jnp.concatenate([first, second], axis=0)


def solution(mesh):
    fine = Mesh(mesh.devices.reshape(16, 2, 2, 2, 4), AXES)
    return jax.shard_map(
        shards,
        mesh=fine,
        in_specs=(P(AXES, None, None), P(AXES, None), P(("z", "xhi", "core"), None)),
        out_specs=P(AXES, None, None),
        check_vma=False,
    )
```

```python
import functools

import jax
import jax.numpy as jnp
from jax import lax
from jax.experimental import pallas as pl
from jax.experimental.pallas import tpu as pltpu
from jax.sharding import Mesh
from jax.sharding import PartitionSpec as P

NB = 1536
NZ = 16
AXES = ("z", "xhi", "core", "xlo", "y")
LEFT = (0, -4, 4, 0)
RIGHT = (0, 0, -4, -4)


def flat(z, xhi, core, xlo, y):
    return (((z % NZ * 2 + xhi) * 2 + core) * 2 + xlo) * 4 + y


def coords():
    for z in range(NZ):
        for xhi in range(2):
            for core in range(2):
                for xlo in range(2):
                    for y in range(4):
                        yield z, xhi, core, xlo, y


def send(value, target):
    pairs = []
    for at in coords():
        to = target(*at)
        if to is not None:
            pairs.append((flat(*at), flat(*to)))
    return lax.ppermute(value, AXES, pairs)


def other_core(z, xhi, core, xlo, y):
    return z, xhi, 1 - core, xlo, y


def ring_z(z, xhi, core, xlo, y):
    return (z - 1 if core == 0 else z + 1), xhi, core, xlo, y


def plane_step(phase, offset):
    def target(z, xhi, core, xlo, y):
        if phase == core:
            return z, xhi, core, xlo, (y + offset) % 4
        x = (xhi * 2 + xlo + offset) % 4
        return z, x // 2, core, x % 2, y

    return target


def home(chunk, same):
    def target(z, xhi, core, xlo, y):
        c = ((0, 3), (1, 2))[chunk][xhi]
        if (core == c % 2) != same:
            return None
        return z + LEFT[c], xhi, c % 2, xlo, y

    return target


def sort_kernel(ids_ref, blocks_ref, out_ref):
    count = blocks_ref.shape[0]
    keys = []
    for s in range(count):
        row = ids_ref[0, s]
        keys.append(jnp.where(row >= 0, row * NB + ids_ref[1, s], 2**30 + s))
    for s in range(count):
        rank = jnp.int32(0)
        for o in range(count):
            if o != s:
                rank = rank + jnp.where(keys[o] < keys[s], 1, 0)
        out_ref[rank] = blocks_ref[s]


def sort_blocks(block_ids, blocks):
    return pl.pallas_call(
        sort_kernel,
        out_shape=jax.ShapeDtypeStruct(blocks.shape, blocks.dtype),
        in_specs=[
            pl.BlockSpec(memory_space=pltpu.SMEM),
            pl.BlockSpec(memory_space=pltpu.VMEM),
        ],
        out_specs=pl.BlockSpec(memory_space=pltpu.VMEM),
        name="sort_blocks",
    )(block_ids.T, blocks)


REACH = 4


def split_into(panel, at, quarter, hi_ref, lo_ref):
    for rho in range(4):
        for col in range(2):
            x = panel[2 * rho + col]
            hi = x.astype(jnp.bfloat16)
            lo = (x - hi.astype(jnp.float32)).astype(jnp.bfloat16)
            lanes = pl.ds(pl.multiple_of(quarter * 256 + col * 128, 128), 128)
            hi_ref[at, rho * 128 : (rho + 1) * 128, lanes] = hi
            lo_ref[at, rho * 128 : (rho + 1) * 128, lanes] = lo


def split_pair(core, panels, hi_ref, lo_ref):
    ahead = 1 - core
    places = ((ahead, core), (ahead, 1 - core), (1 - ahead, 1 - core), (1 - ahead, core))
    for panel, (at, quarter) in zip(panels, places):
        split_into(panel, at, quarter, hi_ref, lo_ref)


def split_kernel(where_ref, *refs):
    core = where_ref[0]
    *panels, hi_ref, lo_ref = refs
    if len(panels) == 2:
        split_into(panels[0], 0, core, hi_ref, lo_ref)
        split_into(panels[1], 0, 1 - core, hi_ref, lo_ref)
    else:
        split_pair(core, panels, hi_ref, lo_ref)


def split_rows(where, *panels):
    vmem = pl.BlockSpec(memory_space=pltpu.VMEM)
    smem = pl.BlockSpec(memory_space=pltpu.SMEM)
    return pl.pallas_call(
        split_kernel,
        out_shape=[jax.ShapeDtypeStruct((len(panels) // 2, 512, 512), jnp.bfloat16)] * 2,
        in_specs=[smem] + [vmem] * len(panels),
        out_specs=[vmem] * 2,
        compiler_params=pltpu.CompilerParams(vmem_limit_bytes=8 << 20),
        name=f"split_{len(panels)}",
    )(where, *panels)


def chunk_kernel(chunk, where_ref, codes_ref, *refs):
    core = where_ref[0]
    place = where_ref[1]
    xhi = place // 8
    count = 2 * REACH + 2
    rows_hi, rows_lo = refs[:count:2], refs[1:count:2]
    outs = refs[count : count + 4]
    [res_ref] = refs[count + 4 :]

    def row(offset):
        at = int(offset > 0)
        return rows_hi[abs(offset)].at[at], rows_lo[abs(offset)].at[at]

    def times(a, b):
        return lax.dot_general(
            a[...], b[...], (((1,), (1,)), ((), ())), preferred_element_type=jnp.float32
        )

    lists = ((0, 3), (1, 2))[chunk]
    held = [(c % 2 ^ core) + 2 * (c // 2 ^ xhi) for c in lists]
    for far, c in enumerate(lists):
        left_hi, left_lo = row(LEFT[c])
        for step in range(4):
            right_hi, right_lo = row(RIGHT[c] + step)
            res_ref[far * 4 + step] = (
                times(left_hi, right_hi) + times(left_hi, right_lo) + times(left_lo, right_hi)
            )
    x, y = place // 4, place % 4
    for offset in range(4):

        def pick(index, carry, offset=offset):
            after_that = index // 4
            to_x = (x + jnp.where(core == 0, after_that, offset)) % 4
            to_y = (y + jnp.where(core == 0, offset, after_that)) % 4
            far = to_x // 2
            slot = (to_x % 2 * 4 + to_y) * 8 + core * 4 + index % 4
            code = codes_ref[jnp.where(far == 0, held[0], held[1]), slot]
            good = code >= 0
            code = jnp.maximum(code, 0)
            rows = pl.ds(pl.multiple_of(code // 16 * 128, 128), 128)
            cols = pl.ds(pl.multiple_of(code % 4 * 128, 128), 128)
            block = res_ref[far * 4 + code // 4 % 4, rows, cols]
            outs[offset][index] = jnp.where(good, block, jnp.float32(0.0))
            return carry

        lax.fori_loop(0, 16, pick, 0, unroll=4)


def chunk_products(chunk, where, codes, split):
    vmem = pl.BlockSpec(memory_space=pltpu.VMEM)
    smem = pl.BlockSpec(memory_space=pltpu.SMEM)
    return pl.pallas_call(
        functools.partial(chunk_kernel, chunk),
        out_shape=[jax.ShapeDtypeStruct((16, 128, 128), jnp.float32)] * 4,
        in_specs=[smem] * 2 + [vmem] * len(split),
        out_specs=[vmem] * 4,
        scratch_shapes=[pltpu.VMEM((8, 512, 512), jnp.float32)],
        compiler_params=pltpu.CompilerParams(vmem_limit_bytes=20 << 20),
        name=f"products_{chunk}",
    )(where, codes, *split)


def slot_codes(out_ids, row, col):
    i = out_ids[:, 0]
    j = out_ids[:, 1]
    good = (i >= 0) & (j >= 0)
    same_j = (j[None, :] == j[:, None]) & good[None, :]
    same_i = (i[None, :] == i[:, None]) & good[None, :]
    group = lax.rem(j, NZ)
    left = jnp.sum((same_j & (i[None, :] < i[:, None])).astype(jnp.int32), axis=1)
    right = jnp.sum(
        (same_i & (group[None, :] == group[:, None]) & (j[None, :] < j[:, None])).astype(jnp.int32),
        axis=1,
    )
    step = lax.rem(group - row - 4 * col + 8 * NZ, NZ)
    return jnp.where(good, left * 16 + step * 4 + right, -1)


def after(value, *others):
    return lax.optimization_barrier((value, *others))[0]


def reduce_plane(pieces, others=(), late=(), third=()):
    received = [None] * 4
    for offset in (2, 1, 3):
        piece = pieces[offset]
        if third and offset == 3:
            piece = after(piece, *third)
        received[offset] = send(piece, plane_step(0, offset))
    if others:
        received[1:] = lax.optimization_barrier((*others, *received[1:]))[-3:]
    count = pieces[0].shape[0] // 4
    total = [
        sum((received[o][n * count : (n + 1) * count] for o in (1, 2, 3)), pieces[0][n * count : (n + 1) * count])
        for n in range(4)
    ]
    arrived = [send(total[offset], plane_step(1, offset)) for offset in (2, 1, 3)]
    if late:
        arrived = lax.optimization_barrier((*late, *arrived))[-3:]
    return total[0] + arrived[0] + arrived[1] + arrived[2], arrived


def bring_home(part):
    return send(part, home(1, True)), send(part, home(1, False))


def to_place(z, xhi, core, xlo, y):
    return z - LEFT[xhi * 2 + core], xhi, core, xlo, y


def other_xhi(z, xhi, core, xlo, y):
    return z, 1 - xhi, core, xlo, y


def shards(blocks, block_ids, out_ids):
    z = lax.axis_index("z")
    xhi = lax.axis_index("xhi")
    core = lax.axis_index("core")
    x = xhi * 2 + lax.axis_index("xlo")
    where = jnp.stack([core, x * 4 + lax.axis_index("y")]).astype(jnp.int32)

    placed = send(out_ids, to_place)
    col = xhi * 2 + core
    left = jnp.where(col == 1, LEFT[1], jnp.where(col == 2, LEFT[2], 0))
    codes = slot_codes(placed, z + left, col)[None]
    chip_codes = jnp.concatenate([codes, send(codes, other_core)], axis=0)
    codes = jnp.concatenate([chip_codes, send(chip_codes, other_xhi)], axis=0)

    mine_a = [sort_blocks(block_ids, blocks)]
    mine_b = [send(mine_a[0], other_core)]
    split = [split_rows(where, mine_a[0], mine_b[0])]
    their_a, their_b = [None], [None]
    for k in range(1, REACH + 1):
        next_a, next_b = mine_a[-1], mine_b[-1]
        if k == 2:
            next_b = after(next_b, placed)
        if k == 3:
            next_b = after(next_b, chip_codes)
        if k > 2:
            next_a = after(next_a, their_a[k - 2])
            next_b = after(next_b, split[k - 2][0])
        mine_a.append(send(next_a, ring_z))
        mine_b.append(send(next_b, ring_z))
        their_a.append(send(mine_a[k], other_core))
        swap_b = mine_b[k] if k < REACH else after(mine_b[k], codes)
        their_b.append(send(swap_b, other_core))
        split.append(split_rows(where, mine_a[k], mine_b[k], their_a[k], their_b[k]))
    split = [part for pair in split for part in pair]

    pieces = chunk_products(1, where, codes, split)
    wide, arrived = reduce_plane(pieces)
    far_same, far_cross = bring_home(wide)
    pieces = chunk_products(0, where, after(codes, pieces[0]), split)
    near, _ = reduce_plane(pieces, [wide], (far_same, far_cross), ())
    near_cross = send(near, home(0, False))

    same = jnp.where(core == xhi, near, far_same)
    cross = jnp.where(core == xhi, near_cross, far_cross)
    first = jnp.where(core == 0, same, cross)
    second = jnp.where(core == 0, cross, same)
    return jnp.concatenate([first, second], axis=0)


def solution(mesh):
    fine = Mesh(mesh.devices.reshape(16, 2, 2, 2, 4), AXES)
    return jax.shard_map(
        shards,
        mesh=fine,
        in_specs=(P(AXES, None, None), P(AXES, None), P(("z", "xhi", "core"), None)),
        out_specs=P(AXES, None, None),
        check_vma=False,
    )
```
